512 devices in a mesh: occ: 64 (over x, y, core), aux: 8 (over z).
Axes of the slice: x: 4, y: 8, z: 8, core: 2. Of those that a mesh axis runs over, the one named last changes fastest.
Arguments:
- ao_blocks: bfloat16 [256, 256, 8192], P('occ', None, 'aux'), may hold values from -0.59765625 to 0.59765625
- pno_coef: bfloat16 [1024, 256, 200], P('occ'), may hold values from -0.375 to 0.375
- pno_energy: float32 [1024, 200], P('occ'), may hold values from 0.3 to 3
- occ_energy: float32 [256], replicated, may hold values from -1.5 to -0.3
- pair_partner: int32 [1024], P('occ'), may hold values from 0 to 255, as said below
- pno_count: int32 [1024], P('occ'), may hold values from 40 to 200, as said below
Outputs:
- amplitudes: float32 [1024, 200, 200], P(('occ', 'aux'))
- orbital_pair_energy: float32 [256], P('occ')
The draws below stay inside these ranges and needn't reach their ends.
Inputs may be any that keep to these rules, and one draw needn't show every extreme that they name: pair_partner[s] differs from own(s) and is an orbital owned by the same index of occ as own(s), or by the index just below or just above it. `pno_count`: every count is a multiple of 8; in every block of 16 pairs one count is 200 and one is 40.
All inputs are finite; a program needn't handle non-finite values.
Results may differ from the reference program's by a relative error of at most 0.0041.
Values may be sent and summed in bfloat16 or wider, within the bound.
A program may use at most 128 MiB of HBM per device.

```python
import math
import jax
import jax.numpy as jnp
from jax import lax

NV = 256
PMAX = 200
PPO = 4
ORB_DEV = 4
PAIR_DEV = 16
NOCC = 256
PAIRS = 1024
AUX = 8192


def draw_pair_partner(key, part):
    pair_ids = jnp.arange(PAIRS, dtype=jnp.int32)
    owner = pair_ids // PAIR_DEV
    own_orbital = owner * ORB_DEV + pair_ids % PAIR_DEV // PPO
    lowest = jnp.maximum(0, (owner - 1) * ORB_DEV)
    highest = jnp.minimum(NOCC, (owner + 2) * ORB_DEV)
    picked = jax.random.randint(jax.random.fold_in(key, 11), (PAIRS,), 0, highest - lowest - 1)
    partner = lowest + picked
    partner = partner + (partner >= own_orbital).astype(jnp.int32)
    return partner.astype(jnp.int32)


def draw_pno_count(key, part):
    pair_ids = jnp.arange(PAIRS, dtype=jnp.int32)
    levels = (PMAX - 40) // 8 + 1
    counts = 40 + 8 * jax.random.randint(jax.random.fold_in(key, 23), (PAIRS,), 0, levels)
    counts = jnp.where(pair_ids % PAIR_DEV == 0, PMAX, counts)
    counts = jnp.where(pair_ids % PAIR_DEV == 1, 40, counts)
    return counts.astype(jnp.int32)


def shard_levels(own_key, extent, pieces, smallest, top_value):
    gain, own = 1.0, jax.random.fold_in(own_key, 6)
    for position, blocks in pieces:
        draws = jnp.exp(jax.random.uniform(jax.random.fold_in(own, position), (blocks,), jnp.float32, smallest / len(pieces), top_value / len(pieces)))
        gain = gain * jnp.repeat(draws, extent[position] // blocks).reshape([-1 if axis == position else 1 for axis in range(len(extent))])
    return gain


def centred(key, extent, scale, most, split=(), kind=jnp.bfloat16):
    result = jax.random.normal(key, extent, jnp.float32) * scale
    if len(split) > 0:
        result = shard_levels(key, extent, split, -0.22, 0.18) * result
    return jnp.clip(result, min=-most, max=most).astype(kind)


def setup_inputs(seed: int = 0) -> dict:
    key_list = jax.random.split(jax.random.key(seed), 7)
    return {
        "ao_blocks": centred(key_list[0], (NOCC, NV, AUX), 0.1, 0.59765625, ((0, 64), (2, 8))),
        "pno_coef": centred(key_list[1], (PAIRS, NV, PMAX), NV ** -0.5, 0.375, ((0, 64),)),
        "pno_energy": jnp.clip(jnp.exp(math.log(3.0) - 2.3025851 * jax.random.uniform(key_list[2], (PAIRS, PMAX), jnp.float32) ** shard_levels(key_list[2], (PAIRS, PMAX), ((0, 64),), -0.2, 0.2)), 0.3, 3.0),
        "occ_energy": jnp.clip(jax.random.uniform(key_list[3], (NOCC,), jnp.float32, -1.5, -0.3), -1.5, -0.3),
        "pair_partner": draw_pair_partner(jax.random.fold_in(key_list[6], 71), 0),
        "pno_count": draw_pno_count(jax.random.fold_in(key_list[6], 71), 0),
    }


def reference(ao_blocks, pno_coef, pno_energy, occ_energy, pair_partner, pno_count):
    pair_ids = jnp.arange(PAIRS, dtype=jnp.int32)
    own_orbital = ((pair_ids // PAIR_DEV) * ORB_DEV + (pair_ids % PAIR_DEV) // PPO).astype(jnp.int32)
    columns = jnp.arange(PMAX, dtype=jnp.int32)
    kept_mask = (columns[None, :] < pno_count[:, None]).astype(jnp.bfloat16)
    masked_coef = pno_coef * kept_mask[:, None, :]

    def pair_terms(items):
        coef_row, own_id, partner_id, energies = items
        proj_own = jnp.dot(coef_row.T, ao_blocks[own_id], preferred_element_type=jnp.float32).astype(jnp.bfloat16)
        proj_partner = jnp.dot(coef_row.T, ao_blocks[partner_id], preferred_element_type=jnp.float32).astype(jnp.bfloat16)
        exchange = jnp.dot(proj_own, proj_partner.T, preferred_element_type=jnp.float32)
        denominator = energies[:, None] + energies[None, :] - occ_energy[own_id] - occ_energy[partner_id]
        amplitude = -exchange / denominator
        energy = jnp.sum((2.0 * exchange - exchange.T) * amplitude)
        return amplitude, energy

    amplitudes, pair_energy = lax.map(pair_terms, (masked_coef, own_orbital, pair_partner, pno_energy))
    orbital = jnp.zeros((NOCC,), jnp.float32)
    orbital = orbital.at[own_orbital].add(0.5 * pair_energy)
    orbital = orbital.at[pair_partner].add(0.5 * pair_energy)
    return amplitudes, orbital
```

```python
import functools

import jax
import jax.numpy as jnp
from jax import lax
from jax.experimental import pallas as pl
from jax.experimental.pallas import tpu as pltpu
from jax.sharding import PartitionSpec as P

MESH = pl.DeviceIdType.MESH
CHUNKS = 4
LANES = 128
F32 = jnp.float32
BF16 = jnp.bfloat16

ORDER = (
    (4, 0), (4, 1), (3, 1), (-3, 0),
    (3, 0), (-3, 1), (2, 0), (-2, 1),
    (2, 1), (-2, 0), (1, 0), (-1, 1),
    (1, 1), (-1, 0), (0, 0), (0, 1),
)
CHAINS = (
    (1, (0, 4, 6, 10)),
    (-1, (1, 5, 7, 11)),
    (1, (2, 8, 12)),
    (-1, (3, 9, 13)),
)
MESSAGES = 14


def nt_dot(left, right):
    return lax.dot_general(
        left, right, (((1,), (1,)), ((), ())), preferred_element_type=F32
    )


def kernel(
    occ_size, aux_size, partner, counts, occ_energy, energies, ao, coef,
    amp_out, orb_out,
    win0, win1, win2, win3, coefs, coef_t, own_proj, sums, parcel, landed,
    amp, gift, gifts, level, levels,
    local_sem, ao_send, ao_recv, chain_send, chain_recv, amp_sem,
    gift_send, gift_recv, level_send, level_recv,
):
    windows = (win0, win1, win2, win3)
    occ_me, aux_me = lax.axis_index("occ"), lax.axis_index("aux")
    right = lax.rem(occ_me + 1, occ_size)
    left = lax.rem(occ_me + occ_size - 1, occ_size)
    orbs = ao.shape[0]
    virtuals = ao.shape[1]
    width = ao.shape[2] // CHUNKS
    pairs, _, pnos = coef.shape
    per_orbital = pairs // orbs
    rows = own_proj.shape[1]

    def aux_at(distance):
        return lax.rem(aux_me + distance + aux_size, aux_size)

    barrier = pltpu.get_barrier_semaphore()
    for place in ((left, aux_me), (right, aux_me), (occ_me, aux_at(1)), (occ_me, aux_at(-1))):
        pl.semaphore_signal(barrier, inc=1, device_id=place, device_id_type=MESH)

    fetch_coef = pltpu.make_async_copy(coef, coefs, local_sem.at[CHUNKS])
    fetch_coef.start()
    fetches = []
    for k in range(CHUNKS):
        fetch = pltpu.make_async_copy(
            ao.at[:, :, pl.ds(k * width, width)],
            windows[k].at[pl.ds(orbs, orbs)],
            local_sem.at[k],
        )
        fetch.start()
        fetches.append(fetch)

    pl.semaphore_wait(barrier, 4)

    moves = []
    for k in range(CHUNKS):
        for side, (target, slot) in enumerate(((right, 0), (left, 2 * orbs))):
            move = pltpu.make_async_remote_copy(
                src_ref=ao.at[:, :, pl.ds(k * width, width)],
                dst_ref=windows[k].at[pl.ds(slot, orbs)],
                send_sem=ao_send.at[side, k],
                recv_sem=ao_recv.at[side, k],
                device_id=(target, aux_me),
                device_id_type=MESH,
            )
            move.start()
            moves.append(move)

    fetch_coef.wait()
    lanes = lax.broadcasted_iota(jnp.int32, (virtuals, pnos), 1)

    def turn(s, carry):
        kept = (lanes < counts[s]).astype(F32)
        flipped = (coefs[s].astype(F32) * kept).T
        coef_t[s] = jnp.zeros(coef_t.shape[1:], BF16)
        coef_t[s, :pnos] = flipped.astype(BF16)
        return carry

    lax.fori_loop(0, pairs, turn, 0)

    for k in range(CHUNKS):
        fetches[k].wait()

        def project(s, carry):
            block = windows[k][orbs + s // per_orbital]
            own = jnp.dot(coef_t[s, :rows], block, preferred_element_type=F32)
            own_proj[s, :, k * width:(k + 1) * width] = own.astype(BF16)
            return carry

        lax.fori_loop(0, pairs, project, 0, unroll=2)

    first_slot = (occ_me - 1) * orbs

    def slot_of(s):
        return jnp.clip(partner[s] - first_slot, 0, 3 * orbs - 1)

    def partial(s, k):
        block = windows[k][slot_of(s)]
        other = jnp.dot(coef_t[s], block, preferred_element_type=F32).astype(BF16)
        return nt_dot(own_proj[s, :, k * width:(k + 1) * width], other)

    for k in range(CHUNKS):
        moves[2 * k].wait_recv()
        moves[2 * k + 1].wait_recv()

        def accumulate(s, carry):
            if k == 0:
                sums[s] = partial(s, k)
            else:
                sums[s] = sums[s] + partial(s, k)
            return carry

        lax.fori_loop(0, pairs, accumulate, 0, unroll=2)

    def pair_at(position):
        distance, place = ORDER[position]
        return 2 * aux_at(distance) + place

    messages = {}

    def forward(chain, step):
        direction, positions = CHAINS[chain]
        number = sum(len(CHAINS[c][1]) for c in range(chain)) + step
        total = sums[pair_at(positions[step])]
        if step > 0:
            messages[chain, step - 1].wait_recv()
            total = total + landed[number - 1].astype(F32)
        parcel[number] = total.astype(BF16)
        message = pltpu.make_async_remote_copy(
            src_ref=parcel.at[number],
            dst_ref=landed.at[number],
            send_sem=chain_send.at[number],
            recv_sem=chain_recv.at[number],
            device_id=(occ_me, aux_at(direction)),
            device_id_type=MESH,
        )
        message.start()
        messages[chain, step] = message

    for step in range(4):
        for chain in range(4):
            if step < len(CHAINS[chain][1]):
                forward(chain, step)

    def closed(chain):
        steps = len(CHAINS[chain][1])
        number = sum(len(CHAINS[c][1]) for c in range(chain)) + steps - 1
        messages[chain, steps - 1].wait_recv()
        return landed[number].astype(F32)

    lane = lax.broadcasted_iota(jnp.int32, gift.shape, 1)
    spread = jnp.zeros(gift.shape, F32)
    writes = []
    for place, (long_chain, short_chain) in enumerate(((0, 3), (1, 2))):
        s = 2 * aux_me + place
        short = closed(short_chain)
        total = (sums[s] + short + closed(long_chain))[:pnos, :pnos]
        slot = slot_of(s)
        own_slot = orbs + s // per_orbital
        shift = occ_energy[first_slot + own_slot] + occ_energy[partner[s]]
        row = jnp.broadcast_to(energies[pl.ds(s, 1), :], (pnos, pnos))
        denominator = row + row.T - shift
        amplitude = -total / denominator
        amp[place] = amplitude
        write = pltpu.make_async_copy(amp.at[place], amp_out.at[place], amp_sem.at[place])
        write.start()
        writes.append(write)
        energy = jnp.sum((2.0 * total - total.T) * amplitude, axis=0, keepdims=True)
        energy = 0.5 * jnp.sum(energy, axis=1, keepdims=True)
        hits = (lane == own_slot).astype(F32) + (lane == slot).astype(F32)
        spread = spread + hits * energy

    gift[...] = spread
    passes = []
    for side, target in enumerate((right, left)):
        passed = pltpu.make_async_remote_copy(
            src_ref=gift,
            dst_ref=gifts.at[side],
            send_sem=gift_send.at[side],
            recv_sem=gift_recv.at[side],
            device_id=(target, aux_me),
            device_id_type=MESH,
        )
        passed.start()
        passes.append(passed)
    for passed in passes:
        passed.wait_recv()
    mine = (
        pltpu.roll(gifts[0], LANES - 2 * orbs, 1)
        + pltpu.roll(spread, LANES - orbs, 1)
        + gifts[1]
    )
    level[...] = mine
    levels[aux_me] = mine
    for distance in range(1, aux_size):
        passed = pltpu.make_async_remote_copy(
            src_ref=level,
            dst_ref=levels.at[aux_me],
            send_sem=level_send.at[distance],
            recv_sem=level_recv.at[distance],
            device_id=(occ_me, aux_at(distance)),
            device_id_type=MESH,
        )
        passed.start()
        passes.append(passed)
    for passed in passes[2:]:
        passed.wait_recv()
    whole = levels[0]
    for place in range(1, aux_size):
        whole = whole + levels[place]
    orb_out[...] = whole

    for move in moves:
        move.wait_send()
    for message in messages.values():
        message.wait_send()
    for passed in passes:
        passed.wait_send()
    for write in writes:
        write.wait()


def shards(mesh, ao_blocks, pno_coef, pno_energy, occ_energy, pair_partner, pno_count):
    orbs, virtuals, aux_block = ao_blocks.shape
    pairs, _, pnos = pno_coef.shape
    width = aux_block // CHUNKS
    occ_size, aux_size = mesh.shape["occ"], mesh.shape["aux"]
    rows = -(-pnos // 16) * 16
    padded = -(-pnos // LANES) * LANES
    share = pairs // aux_size
    smem = pl.BlockSpec(memory_space=pltpu.SMEM)
    vmem = pl.BlockSpec(memory_space=pltpu.VMEM)
    anywhere = pl.BlockSpec(memory_space=pl.ANY)
    dma = pltpu.SemaphoreType.DMA
    amplitudes, orbital = pl.pallas_call(
        functools.partial(kernel, occ_size, aux_size),
        out_shape=(
            jax.ShapeDtypeStruct((share, pnos, pnos), F32),
            jax.ShapeDtypeStruct((8, LANES), F32),
        ),
        in_specs=[smem, smem, smem, vmem, anywhere, anywhere],
        out_specs=(anywhere, vmem),
        scratch_shapes=[pltpu.VMEM((3 * orbs, virtuals, width), BF16)] * CHUNKS
        + [
            pltpu.VMEM((pairs, virtuals, pnos), BF16),
            pltpu.VMEM((pairs, padded, virtuals), BF16),
            pltpu.VMEM((pairs, rows, aux_block), BF16),
            pltpu.VMEM((pairs, rows, padded), F32),
            pltpu.VMEM((MESSAGES, rows, padded), BF16),
            pltpu.VMEM((MESSAGES, rows, padded), BF16),
            pltpu.VMEM((share, pnos, pnos), F32),
            pltpu.VMEM((8, LANES), F32),
            pltpu.VMEM((2, 8, LANES), F32),
            pltpu.VMEM((8, LANES), F32),
            pltpu.VMEM((aux_size, 8, LANES), F32),
            dma((CHUNKS + 1,)),
            dma((2, CHUNKS)),
            dma((2, CHUNKS)),
            dma((MESSAGES,)),
            dma((MESSAGES,)),
            dma((share,)),
            dma((2,)),
            dma((2,)),
            dma((aux_size,)),
            dma((aux_size,)),
        ],
        compiler_params=pltpu.CompilerParams(
            collective_id=0, has_side_effects=True, vmem_limit_bytes=60 * 1024 * 1024
        ),
    )(pair_partner, pno_count, occ_energy, pno_energy, ao_blocks, pno_coef)
    return amplitudes, orbital[0, :orbs]


def solution(mesh):
    return jax.shard_map(
        functools.partial(shards, mesh),
        mesh=mesh,
        in_specs=(
            P("occ", None, "aux"),
            P("occ", None, None),
            P("occ", None),
            P(),
            P("occ"),
            P("occ"),
        ),
        out_specs=(P(("occ", "aux"), None, None), P("occ")),
        check_vma=False,
    )
```

```python
import functools

import jax
import jax.numpy as jnp
from jax import lax
from jax.experimental import pallas as pl
from jax.experimental.pallas import tpu as pltpu
from jax.sharding import PartitionSpec as P

MESH = pl.DeviceIdType.MESH
CHUNKS = 4
LANES = 128
F32 = jnp.float32
BF16 = jnp.bfloat16

ORDER = (
    (4, 0), (4, 1), (3, 1), (-3, 0),
    (3, 0), (-3, 1), (2, 0), (-2, 1),
    (2, 1), (-2, 0), (1, 0), (-1, 1),
    (1, 1), (-1, 0), (0, 0), (0, 1),
)
CHAINS = (
    (1, (0, 4, 6, 10)),
    (-1, (1, 5, 7, 11)),
    (1, (2, 8, 12)),
    (-1, (3, 9, 13)),
)
MESSAGES = 14


def nt_dot(left, right):
    return lax.dot_general(
        left, right, (((1,), (1,)), ((), ())), preferred_element_type=F32
    )


def kernel(
    occ_size, aux_size, partner, counts, occ_energy, energies, ao, coef,
    amp_out, orb_out,
    win0, win1, win2, win3, coefs, coef_t, own_proj, sums, parcel, landed,
    amp, gift, gifts, level, levels,
    local_sem, ao_send, ao_recv, chain_send, chain_recv, amp_sem,
    gift_send, gift_recv, level_send, level_recv,
):
    windows = (win0, win1, win2, win3)
    occ_me, aux_me = lax.axis_index("occ"), lax.axis_index("aux")
    right = lax.rem(occ_me + 1, occ_size)
    left = lax.rem(occ_me + occ_size - 1, occ_size)
    orbs = ao.shape[0]
    virtuals = ao.shape[1]
    width = ao.shape[2] // CHUNKS
    pairs, pnos, _ = coef.shape
    per_orbital = pairs // orbs
    rows = own_proj.shape[1]

    def aux_at(distance):
        return lax.rem(aux_me + distance + aux_size, aux_size)

    barrier = pltpu.get_barrier_semaphore()
    for place in ((left, aux_me), (right, aux_me), (occ_me, aux_at(1)), (occ_me, aux_at(-1))):
        pl.semaphore_signal(barrier, inc=1, device_id=place, device_id_type=MESH)

    fetch_coef = pltpu.make_async_copy(coef, coefs, local_sem.at[CHUNKS])
    fetch_coef.start()
    fetches = []
    for k in range(CHUNKS):
        fetch = pltpu.make_async_copy(
            ao.at[:, :, pl.ds(k * width, width)],
            windows[k].at[pl.ds(orbs, orbs)],
            local_sem.at[k],
        )
        fetch.start()
        fetches.append(fetch)

    pl.semaphore_wait(barrier, 4)

    moves = []
    for k in range(CHUNKS):
        for side, (target, slot) in enumerate(((right, 0), (left, 2 * orbs))):
            move = pltpu.make_async_remote_copy(
                src_ref=ao.at[:, :, pl.ds(k * width, width)],
                dst_ref=windows[k].at[pl.ds(slot, orbs)],
                send_sem=ao_send.at[side, k],
                recv_sem=ao_recv.at[side, k],
                device_id=(target, aux_me),
                device_id_type=MESH,
            )
            move.start()
            moves.append(move)

    fetch_coef.wait()
    padded = coef_t.shape[1]
    whole_rows = pnos // 16 * 16
    places = lax.broadcasted_iota(jnp.int32, (pnos, virtuals), 0)

    def mask(s, carry):
        kept = jnp.where(places < counts[s], coefs[s].astype(F32), 0.0)
        coef_t[s, whole_rows:] = jnp.zeros((padded - whole_rows, virtuals), BF16)
        coef_t[s, :pnos] = kept.astype(BF16)
        return carry

    lax.fori_loop(0, pairs, mask, 0)

    for k in range(CHUNKS):
        fetches[k].wait()

        def project(s, carry):
            block = windows[k][orbs + s // per_orbital]
            own = jnp.dot(coef_t[s, :rows], block, preferred_element_type=F32)
            own_proj[s, :, k * width:(k + 1) * width] = own.astype(BF16)
            return carry

        lax.fori_loop(0, pairs, project, 0, unroll=2)

    first_slot = (occ_me - 1) * orbs

    def slot_of(s):
        return jnp.clip(partner[s] - first_slot, 0, 3 * orbs - 1)

    def partial(s, k):
        block = windows[k][slot_of(s)]
        other = jnp.dot(coef_t[s], block, preferred_element_type=F32).astype(BF16)
        return nt_dot(own_proj[s, :, k * width:(k + 1) * width], other)

    for k in range(CHUNKS):
        moves[2 * k].wait_recv()
        moves[2 * k + 1].wait_recv()

        def accumulate(s, carry):
            if k == 0:
                sums[s] = partial(s, k)
            else:
                sums[s] = sums[s] + partial(s, k)
            return carry

        lax.fori_loop(0, pairs, accumulate, 0, unroll=2)

    def pair_at(position):
        distance, place = ORDER[position]
        return 2 * aux_at(distance) + place

    messages = {}

    def forward(chain, step):
        direction, positions = CHAINS[chain]
        number = sum(len(CHAINS[c][1]) for c in range(chain)) + step
        total = sums[pair_at(positions[step])]
        if step > 0:
            messages[chain, step - 1].wait_recv()
            total = total + landed[number - 1].astype(F32)
        parcel[number] = total.astype(BF16)
        message = pltpu.make_async_remote_copy(
            src_ref=parcel.at[number],
            dst_ref=landed.at[number],
            send_sem=chain_send.at[number],
            recv_sem=chain_recv.at[number],
            device_id=(occ_me, aux_at(direction)),
            device_id_type=MESH,
        )
        message.start()
        messages[chain, step] = message

    for step in range(4):
        for chain in range(4):
            if step < len(CHAINS[chain][1]):
                forward(chain, step)

    def closed(chain):
        steps = len(CHAINS[chain][1])
        number = sum(len(CHAINS[c][1]) for c in range(chain)) + steps - 1
        messages[chain, steps - 1].wait_recv()
        return landed[number].astype(F32)

    lane = lax.broadcasted_iota(jnp.int32, gift.shape, 1)
    spread = jnp.zeros(gift.shape, F32)
    writes = []
    for place, (long_chain, short_chain) in enumerate(((0, 3), (1, 2))):
        s = 2 * aux_me + place
        short = closed(short_chain)
        total = (sums[s] + short + closed(long_chain))[:pnos, :pnos]
        slot = slot_of(s)
        own_slot = orbs + s // per_orbital
        shift = occ_energy[first_slot + own_slot] + occ_energy[partner[s]]
        row = jnp.broadcast_to(energies[pl.ds(s, 1), :], (pnos, pnos))
        denominator = row + row.T - shift
        amplitude = -total / denominator
        amp[place] = amplitude
        write = pltpu.make_async_copy(amp.at[place], amp_out.at[place], amp_sem.at[place])
        write.start()
        writes.append(write)
        energy = jnp.sum((2.0 * total - total.T) * amplitude, axis=0, keepdims=True)
        energy = 0.5 * jnp.sum(energy, axis=1, keepdims=True)
        hits = (lane == own_slot).astype(F32) + (lane == slot).astype(F32)
        spread = spread + hits * energy

    gift[...] = spread
    passes = []
    for side, target in enumerate((right, left)):
        passed = pltpu.make_async_remote_copy(
            src_ref=gift,
            dst_ref=gifts.at[side],
            send_sem=gift_send.at[side],
            recv_sem=gift_recv.at[side],
            device_id=(target, aux_me),
            device_id_type=MESH,
        )
        passed.start()
        passes.append(passed)
    for passed in passes:
        passed.wait_recv()
    mine = (
        pltpu.roll(gifts[0], LANES - 2 * orbs, 1)
        + pltpu.roll(spread, LANES - orbs, 1)
        + gifts[1]
    )
    level[...] = mine
    levels[aux_me] = mine
    for distance in range(1, aux_size):
        passed = pltpu.make_async_remote_copy(
            src_ref=level,
            dst_ref=levels.at[aux_me],
            send_sem=level_send.at[distance],
            recv_sem=level_recv.at[distance],
            device_id=(occ_me, aux_at(distance)),
            device_id_type=MESH,
        )
        passed.start()
        passes.append(passed)
    for passed in passes[2:]:
        passed.wait_recv()
    whole = levels[0]
    for place in range(1, aux_size):
        whole = whole + levels[place]
    orb_out[...] = whole

    for move in moves:
        move.wait_send()
    for message in messages.values():
        message.wait_send()
    for passed in passes:
        passed.wait_send()
    for write in writes:
        write.wait()


def shards(mesh, ao_blocks, pno_coef, pno_energy, occ_energy, pair_partner, pno_count):
    orbs, virtuals, aux_block = ao_blocks.shape
    pairs, _, pnos = pno_coef.shape
    width = aux_block // CHUNKS
    occ_size, aux_size = mesh.shape["occ"], mesh.shape["aux"]
    rows = -(-pnos // 16) * 16
    padded = -(-pnos // LANES) * LANES
    share = pairs // aux_size
    smem = pl.BlockSpec(memory_space=pltpu.SMEM)
    vmem = pl.BlockSpec(memory_space=pltpu.VMEM)
    anywhere = pl.BlockSpec(memory_space=pl.ANY)
    dma = pltpu.SemaphoreType.DMA
    amplitudes, orbital = pl.pallas_call(
        functools.partial(kernel, occ_size, aux_size),
        out_shape=(
            jax.ShapeDtypeStruct((share, pnos, pnos), F32),
            jax.ShapeDtypeStruct((8, LANES), F32),
        ),
        in_specs=[smem, smem, smem, vmem, anywhere, anywhere],
        out_specs=(anywhere, vmem),
        scratch_shapes=[pltpu.VMEM((3 * orbs, virtuals, width), BF16)] * CHUNKS
        + [
            pltpu.VMEM((pairs, pnos, virtuals), BF16),
            pltpu.VMEM((pairs, padded, virtuals), BF16),
            pltpu.VMEM((pairs, rows, aux_block), BF16),
            pltpu.VMEM((pairs, rows, padded), F32),
            pltpu.VMEM((MESSAGES, rows, padded), BF16),
            pltpu.VMEM((MESSAGES, rows, padded), BF16),
            pltpu.VMEM((share, pnos, pnos), F32),
            pltpu.VMEM((8, LANES), F32),
            pltpu.VMEM((2, 8, LANES), F32),
            pltpu.VMEM((8, LANES), F32),
            pltpu.VMEM((aux_size, 8, LANES), F32),
            dma((CHUNKS + 1,)),
            dma((2, CHUNKS)),
            dma((2, CHUNKS)),
            dma((MESSAGES,)),
            dma((MESSAGES,)),
            dma((share,)),
            dma((2,)),
            dma((2,)),
            dma((aux_size,)),
            dma((aux_size,)),
        ],
        compiler_params=pltpu.CompilerParams(
            collective_id=0, has_side_effects=True, vmem_limit_bytes=60 * 1024 * 1024
        ),
    )(
        pair_partner, pno_count, occ_energy, pno_energy, ao_blocks,
        jnp.swapaxes(pno_coef, 1, 2),
    )
    return amplitudes, orbital[0, :orbs]


def solution(mesh):
    return jax.shard_map(
        functools.partial(shards, mesh),
        mesh=mesh,
        in_specs=(
            P("occ", None, "aux"),
            P("occ", None, None),
            P("occ", None),
            P(),
            P("occ"),
            P("occ"),
        ),
        out_specs=(P(("occ", "aux"), None, None), P("occ")),
        check_vma=False,
    )
```

```python
import functools

import jax
import jax.numpy as jnp
from jax import lax
from jax.experimental import pallas as pl
from jax.experimental.pallas import tpu as pltpu
from jax.sharding import PartitionSpec as P

MESH = pl.DeviceIdType.MESH
WIDTHS = (256, 256, 256, 128, 128)
GROUP = 4
LANES = 128
F32 = jnp.float32
BF16 = jnp.bfloat16

ORDER = (
    (4, 0), (4, 1), (3, 1), (-3, 0),
    (3, 0), (-3, 1), (2, 0), (-2, 1),
    (2, 1), (-2, 0), (1, 0), (-1, 1),
    (1, 1), (-1, 0), (0, 0), (0, 1),
)
CHAINS = (
    (1, (0, 4, 6, 10)),
    (-1, (1, 5, 7, 11)),
    (1, (2, 8, 12)),
    (-1, (3, 9, 13)),
)
MESSAGES = 14


def nt_dot(left, right):
    return lax.dot_general(
        left, right, (((1,), (1,)), ((), ())), preferred_element_type=F32
    )


def kernel(
    occ_size, aux_size, partner, counts, occ_energy, energies, ao, coef,
    amp_out, orb_out,
    coef_raw, coef_t, own_proj, sums, parcel, landed, scale, amp, gift, gifts, *rest,
):
    windows = rest[:len(WIDTHS)]
    (
        local_sem, ao_send, ao_recv, chain_send, chain_recv, amp_sem,
        gift_send, gift_recv,
    ) = rest[len(WIDTHS):]
    starts = [sum(WIDTHS[:k]) for k in range(len(WIDTHS))]
    occ_me, aux_me = lax.axis_index("occ"), lax.axis_index("aux")
    right = lax.rem(occ_me + 1, occ_size)
    left = lax.rem(occ_me + occ_size - 1, occ_size)
    orbs = ao.shape[0]
    virtuals = ao.shape[1]
    pairs, pnos, _ = coef.shape
    per_orbital = pairs // orbs
    padded = own_proj.shape[1]
    rows = -(-pnos // 16) * 16
    over = pnos - LANES

    def aux_at(distance):
        return lax.rem(aux_me + distance + aux_size, aux_size)

    barrier = pltpu.get_barrier_semaphore()
    for place in ((left, aux_me), (right, aux_me), (occ_me, aux_at(1)), (occ_me, aux_at(-1))):
        pl.semaphore_signal(barrier, inc=1, device_id=place, device_id_type=MESH)

    fetch_coef = pltpu.make_async_copy(coef, coef_raw, local_sem.at[len(WIDTHS)])
    fetch_coef.start()
    fetches = []
    for k, (start, width) in enumerate(zip(starts, WIDTHS)):
        fetch = pltpu.make_async_copy(
            ao.at[:, :, pl.ds(start, width)],
            windows[k].at[pl.ds(orbs, orbs)],
            local_sem.at[k],
        )
        fetch.start()
        fetches.append(fetch)

    pl.semaphore_wait(barrier, 4)

    moves = []
    for k, (start, width) in enumerate(zip(starts, WIDTHS)):
        for side, (target, slot) in enumerate(((right, 0), (left, 2 * orbs))):
            move = pltpu.make_async_remote_copy(
                src_ref=ao.at[:, :, pl.ds(start, width)],
                dst_ref=windows[k].at[pl.ds(slot, orbs)],
                send_sem=ao_send.at[side, k],
                recv_sem=ao_recv.at[side, k],
                device_id=(target, aux_me),
                device_id_type=MESH,
            )
            move.start()
            moves.append(move)

    fetch_coef.wait()
    whole_rows = pnos // 16 * 16
    places = lax.broadcasted_iota(jnp.int32, (pnos, virtuals), 0)

    def mask(s, carry):
        kept = jnp.where(places < counts[s], coef_raw[s].astype(F32), 0.0)
        coef_t[s, whole_rows:] = jnp.zeros((rows - whole_rows, virtuals), BF16)
        coef_t[s, :pnos] = kept.astype(BF16)
        own_proj[s, rows:] = jnp.zeros((padded - rows, own_proj.shape[2]), BF16)
        return carry

    lax.fori_loop(0, pairs, mask, 0)

    first_slot = (occ_me - 1) * orbs

    def slot_of(s):
        return jnp.clip(partner[s] - first_slot, 0, 3 * orbs - 1)

    def own_slot_of(s):
        return orbs + s // per_orbital

    for place in range(2):
        s = 2 * aux_me + place
        shift = occ_energy[first_slot + own_slot_of(s)] + occ_energy[partner[s]]
        row = jnp.broadcast_to(energies[pl.ds(s, 1), :], (pnos, pnos))
        scale[place] = -1.0 / (row + row.T - shift)

    for k, (start, width) in enumerate(zip(starts, WIDTHS)):
        fetches[k].wait()

        def project(o, carry):
            block = windows[k][orbs + o]
            turned = coef_t[pl.ds(o * per_orbital, per_orbital)]
            own = jnp.dot(
                turned.reshape(per_orbital * rows, virtuals), block, preferred_element_type=F32
            )
            own = own.astype(BF16).reshape(per_orbital, rows, width)
            own_proj[pl.ds(o * per_orbital, per_orbital), :rows, start:start + width] = own
            return carry

        lax.fori_loop(0, orbs, project, 0)

    def partials(group, k):
        start, width = starts[k], WIDTHS[k]
        others = [
            jnp.dot(coef_t[s], windows[k][slot_of(s)], preferred_element_type=F32).astype(BF16)
            for s in group
        ]
        owns = [own_proj[s, :, start:start + width] for s in group]
        tops = [nt_dot(own[:rows], other[:LANES]) for own, other in zip(owns, others)]
        rests = [nt_dot(other[LANES:], own) for own, other in zip(owns, others)]
        return [
            jnp.concatenate([top[:pnos], rest[:over, :LANES], rest[:over, LANES:]], axis=0)
            for top, rest in zip(tops, rests)
        ]

    def arrive(k):
        moves[2 * k].wait_recv()
        moves[2 * k + 1].wait_recv()

    last = len(WIDTHS) - 1
    for k in range(last):
        arrive(k)

        def accumulate(number, carry):
            group = [GROUP * number + i for i in range(GROUP)]
            for s, part in zip(group, partials(group, k)):
                sums[s] = part if k == 0 else sums[s] + part
            return carry

        lax.fori_loop(0, pairs // GROUP, accumulate, 0)

    def pair_at(position):
        distance, place = ORDER[position]
        return 2 * aux_at(distance) + place

    messages = {}

    def number_of(chain, step):
        return sum(len(CHAINS[c][1]) for c in range(chain)) + step

    def send(chain, step, total):
        number = number_of(chain, step)
        parcel[number] = total.astype(BF16)
        message = pltpu.make_async_remote_copy(
            src_ref=parcel.at[number],
            dst_ref=landed.at[number],
            send_sem=chain_send.at[number],
            recv_sem=chain_recv.at[number],
            device_id=(occ_me, aux_at(CHAINS[chain][0])),
            device_id_type=MESH,
        )
        message.start()
        messages[chain, step] = message

    def arrived(chain, step):
        messages[chain, step].wait_recv()
        return landed[number_of(chain, step)].astype(F32)

    arrive(last)
    for first in range(0, pairs, GROUP):
        group = [pair_at(position) for position in range(first, first + GROUP)]
        for i, (s, part) in enumerate(zip(group, partials(group, last))):
            total = sums[s] + part
            if first == 0:
                send(i, 0, total)
            else:
                sums[s] = total

    for step in range(1, 4):
        for chain in range(4):
            if step < len(CHAINS[chain][1]):
                s = pair_at(CHAINS[chain][1][step])
                send(chain, step, sums[s] + arrived(chain, step - 1))

    lane = lax.broadcasted_iota(jnp.int32, gift.shape, 1)
    spread = jnp.zeros(gift.shape, F32)
    writes = []

    def added(terms):
        return jnp.sum(jnp.sum(terms, axis=0, keepdims=True), axis=1, keepdims=True)

    for place, (long_chain, short_chain) in enumerate(((0, 3), (1, 2))):
        s = 2 * aux_me + place
        total = sums[s] + arrived(short_chain, 2) + arrived(long_chain, 3)
        low, left_low = total[:LANES], total[LANES:pnos]
        right_up, high = total[pnos:pnos + over], total[pnos + over:, :over]
        scale_low = scale[place, :LANES, :LANES]
        scale_side = scale[place, LANES:, :LANES]
        scale_high = scale[place, LANES:, LANES:]
        amp_low, amp_high = low * scale_low, high * scale_high
        amp[place, :LANES, :LANES] = amp_low
        amp[place, LANES:, :LANES] = left_low * scale_side
        amp[place, :LANES, LANES:] = (right_up * scale_side).T
        amp[place, LANES:, LANES:] = amp_high.T
        write = pltpu.make_async_copy(amp.at[place], amp_out.at[place], amp_sem.at[place])
        write.start()
        writes.append(write)
        mixed = left_low * (left_low - right_up) + right_up * right_up
        energy = 0.5 * (
            added((2.0 * low - low.T) * amp_low)
            + added((2.0 * high - high.T) * amp_high)
            + added(2.0 * mixed * scale_side)
        )
        hits = (lane == own_slot_of(s)).astype(F32) + (lane == slot_of(s)).astype(F32)
        spread = spread + hits * energy

    gift[...] = spread
    gifts[1, aux_me] = spread
    passes = []
    for distance in range(aux_size):
        for side, target in enumerate((right, occ_me, left)):
            if side == 1 and distance == 0:
                continue
            passed = pltpu.make_async_remote_copy(
                src_ref=gift,
                dst_ref=gifts.at[side, aux_me],
                send_sem=gift_send.at[side, distance],
                recv_sem=gift_recv.at[side, distance],
                device_id=(target, aux_at(distance)),
                device_id_type=MESH,
            )
            passed.start()
            passes.append(passed)
    for passed in passes:
        passed.wait_recv()
    from_left, own, from_right = (
        functools.reduce(lambda a, b: a + b, [gifts[side, z] for z in range(aux_size)])
        for side in range(3)
    )
    orb_out[...] = (
        pltpu.roll(from_left, LANES - 2 * orbs, 1)
        + pltpu.roll(own, LANES - orbs, 1)
        + from_right
    )

    for move in moves:
        move.wait_send()
    for message in messages.values():
        message.wait_send()
    for passed in passes:
        passed.wait_send()
    for write in writes:
        write.wait()


def shards(mesh, ao_blocks, pno_coef, pno_energy, occ_energy, pair_partner, pno_count):
    orbs, virtuals, aux_block = ao_blocks.shape
    pairs, _, pnos = pno_coef.shape
    occ_size, aux_size = mesh.shape["occ"], mesh.shape["aux"]
    rows = -(-pnos // 16) * 16
    padded = -(-pnos // LANES) * LANES
    packed = pnos + 2 * (pnos - LANES)
    share = pairs // aux_size
    chunks = len(WIDTHS)
    smem = pl.BlockSpec(memory_space=pltpu.SMEM)
    vmem = pl.BlockSpec(memory_space=pltpu.VMEM)
    anywhere = pl.BlockSpec(memory_space=pl.ANY)
    dma = pltpu.SemaphoreType.DMA
    amplitudes, orbital = pl.pallas_call(
        functools.partial(kernel, occ_size, aux_size),
        out_shape=(
            jax.ShapeDtypeStruct((share, pnos, pnos), F32),
            jax.ShapeDtypeStruct((8, LANES), F32),
        ),
        in_specs=[smem, smem, smem, vmem, anywhere, anywhere],
        out_specs=(anywhere, vmem),
        scratch_shapes=[
            pltpu.VMEM((pairs, pnos, virtuals), BF16),
            pltpu.VMEM((pairs, rows, virtuals), BF16),
            pltpu.VMEM((pairs, padded, aux_block), BF16),
            pltpu.VMEM((pairs, packed, LANES), F32),
            pltpu.VMEM((MESSAGES, packed, LANES), BF16),
            pltpu.VMEM((MESSAGES, packed, LANES), BF16),
            pltpu.VMEM((share, pnos, pnos), F32),
            pltpu.VMEM((share, pnos, pnos), F32),
            pltpu.VMEM((8, LANES), F32),
            pltpu.VMEM((3, aux_size, 8, LANES), F32),
        ]
        + [pltpu.VMEM((3 * orbs, virtuals, width), BF16) for width in WIDTHS]
        + [
            dma((chunks + 1,)),
            dma((2, chunks)),
            dma((2, chunks)),
            dma((MESSAGES,)),
            dma((MESSAGES,)),
            dma((share,)),
            dma((3, aux_size)),
            dma((3, aux_size)),
        ],
        compiler_params=pltpu.CompilerParams(
            collective_id=0, has_side_effects=True, vmem_limit_bytes=53 * 1024 * 1024
        ),
    )(
        pair_partner, pno_count, occ_energy, pno_energy, ao_blocks,
        jnp.swapaxes(pno_coef, 1, 2),
    )
    return amplitudes, orbital[0, :orbs]


def solution(mesh):
    return jax.shard_map(
        functools.partial(shards, mesh),
        mesh=mesh,
        in_specs=(
            P("occ", None, "aux"),
            P("occ", None, None),
            P("occ", None),
            P(),
            P("occ"),
            P("occ"),
        ),
        out_specs=(P(("occ", "aux"), None, None), P("occ")),
        check_vma=False,
    )
```

```python
import functools

import jax
import jax.numpy as jnp
from jax import lax
from jax.experimental import pallas as pl
from jax.experimental.pallas import tpu as pltpu
from jax.sharding import PartitionSpec as P

MESH = pl.DeviceIdType.MESH
WIDTHS = (256, 256, 256, 128, 128)
GROUP = 4
LANES = 128
F32 = jnp.float32
BF16 = jnp.bfloat16

ORDER = (
    (4, 0), (4, 1), (3, 1), (-3, 0),
    (3, 0), (-3, 1), (2, 0), (-2, 1),
    (2, 1), (-2, 0), (1, 0), (-1, 1),
    (1, 1), (-1, 0), (0, 0), (0, 1),
)
CHAINS = (
    (1, (0, 4, 6, 10)),
    (-1, (1, 5, 7, 11)),
    (1, (2, 8, 12)),
    (-1, (3, 9, 13)),
)
MESSAGES = 14


def nt_dot(left, right):
    return lax.dot_general(
        left, right, (((1,), (1,)), ((), ())), preferred_element_type=F32
    )


def kernel(
    occ_size, aux_size, partner_in, counts_in, occ_energy_in, energies_in, ao, coef,
    amp, orb_out,
    partner, counts, occ_energy, energies, coef_raw, coef_t, own_proj, sums, parcel, landed, scale, gift, gifts, *rest,
):
    windows = rest[:len(WIDTHS)]
    (
        small_sem, local_sem, ao_send, ao_recv, chain_send, chain_recv,
        gift_send, gift_recv,
    ) = rest[len(WIDTHS):]
    starts = [sum(WIDTHS[:k]) for k in range(len(WIDTHS))]
    occ_me, aux_me = lax.axis_index("occ"), lax.axis_index("aux")
    right = lax.rem(occ_me + 1, occ_size)
    left = lax.rem(occ_me + occ_size - 1, occ_size)
    orbs = ao.shape[0]
    virtuals = ao.shape[1]
    pairs, pnos, _ = coef.shape
    per_orbital = pairs // orbs
    padded = own_proj.shape[1]
    rows = -(-pnos // 16) * 16
    over = pnos - LANES

    def aux_at(distance):
        return lax.rem(aux_me + distance + aux_size, aux_size)

    barrier = pltpu.get_barrier_semaphore()
    for place in ((left, aux_me), (right, aux_me), (occ_me, aux_at(1)), (occ_me, aux_at(-1))):
        pl.semaphore_signal(barrier, inc=1, device_id=place, device_id_type=MESH)

    pl.semaphore_wait(barrier, 4)

    moves = []
    for k, (start, width) in enumerate(zip(starts, WIDTHS)):
        for side, (target, slot) in enumerate(((right, 0), (left, 2 * orbs))):
            move = pltpu.make_async_remote_copy(
                src_ref=ao.at[:, :, pl.ds(start, width)],
                dst_ref=windows[k].at[pl.ds(slot, orbs)],
                send_sem=ao_send.at[side, k],
                recv_sem=ao_recv.at[side, k],
                device_id=(target, aux_me),
                device_id_type=MESH,
            )
            move.start()
            moves.append(move)

    smalls = []
    for number, (source, target) in enumerate((
        (counts_in, counts), (partner_in, partner), (occ_energy_in, occ_energy),
        (energies_in, energies), (coef, coef_raw),
    )):
        small = pltpu.make_async_copy(source, target, small_sem.at[number])
        small.start()
        smalls.append(small)
    fetches = []
    for k, (start, width) in enumerate(zip(starts, WIDTHS)):
        fetch = pltpu.make_async_copy(
            ao.at[:, :, pl.ds(start, width)],
            windows[k].at[pl.ds(orbs, orbs)],
            local_sem.at[k],
        )
        fetch.start()
        fetches.append(fetch)

    for small in smalls:
        small.wait()
    whole_rows = pnos // 16 * 16
    places = lax.broadcasted_iota(jnp.int32, (pnos, virtuals), 0)

    def mask(s, carry):
        kept = jnp.where(places < counts[s], coef_raw[s].astype(F32), 0.0)
        coef_t[s, whole_rows:] = jnp.zeros((rows - whole_rows, virtuals), BF16)
        coef_t[s, :pnos] = kept.astype(BF16)
        own_proj[s, rows:] = jnp.zeros((padded - rows, own_proj.shape[2]), BF16)
        return carry

    lax.fori_loop(0, pairs, mask, 0)

    first_slot = (occ_me - 1) * orbs

    def slot_of(s):
        return jnp.clip(partner[s] - first_slot, 0, 3 * orbs - 1)

    def own_slot_of(s):
        return orbs + s // per_orbital

    for place in range(2):
        s = 2 * aux_me + place
        shift = occ_energy[first_slot + own_slot_of(s)] + occ_energy[partner[s]]
        row = jnp.broadcast_to(energies[pl.ds(s, 1), :], (pnos, pnos))
        scale[place] = -1.0 / (row + row.T - shift)

    for k, (start, width) in enumerate(zip(starts, WIDTHS)):
        fetches[k].wait()

        def project(o, carry):
            block = windows[k][orbs + o]
            turned = coef_t[pl.ds(o * per_orbital, per_orbital)]
            own = jnp.dot(
                turned.reshape(per_orbital * rows, virtuals), block, preferred_element_type=F32
            )
            own = own.astype(BF16).reshape(per_orbital, rows, width)
            own_proj[pl.ds(o * per_orbital, per_orbital), :rows, start:start + width] = own
            return carry

        lax.fori_loop(0, orbs, project, 0)

    def partials(group, k):
        start, width = starts[k], WIDTHS[k]
        others = [
            jnp.dot(coef_t[s], windows[k][slot_of(s)], preferred_element_type=F32).astype(BF16)
            for s in group
        ]
        owns = [own_proj[s, :, start:start + width] for s in group]
        tops = [nt_dot(own[:rows], other[:LANES]) for own, other in zip(owns, others)]
        rests = [nt_dot(other[LANES:], own) for own, other in zip(owns, others)]
        return [
            jnp.concatenate([top[:pnos], rest[:over, :LANES], rest[:over, LANES:]], axis=0)
            for top, rest in zip(tops, rests)
        ]

    def arrive(k):
        moves[2 * k].wait_recv()
        moves[2 * k + 1].wait_recv()

    last = len(WIDTHS) - 1
    for k in range(last):
        arrive(k)

        def accumulate(number, carry):
            group = [GROUP * number + i for i in range(GROUP)]
            for s, part in zip(group, partials(group, k)):
                sums[s] = part if k == 0 else sums[s] + part
            return carry

        lax.fori_loop(0, pairs // GROUP, accumulate, 0)

    def pair_at(position):
        distance, place = ORDER[position]
        return 2 * aux_at(distance) + place

    messages = {}

    def number_of(chain, step):
        return sum(len(CHAINS[c][1]) for c in range(chain)) + step

    packed = sums.shape[1]
    middle = -(-packed // 32) * 16
    halves = (pl.ds(0, middle), pl.ds(middle, packed - middle))

    def send(chain, step, half, total):
        number = number_of(chain, step)
        parcel[number, halves[half]] = total.astype(BF16)
        message = pltpu.make_async_remote_copy(
            src_ref=parcel.at[number, halves[half]],
            dst_ref=landed.at[number, halves[half]],
            send_sem=chain_send.at[number, half],
            recv_sem=chain_recv.at[number, half],
            device_id=(occ_me, aux_at(CHAINS[chain][0])),
            device_id_type=MESH,
        )
        message.start()
        messages[chain, step, half] = message

    def arrived(chain, step, half):
        messages[chain, step, half].wait_recv()
        return landed[number_of(chain, step), halves[half]].astype(F32)

    arrive(last)
    for first in range(0, pairs, GROUP):
        group = [pair_at(position) for position in range(first, first + GROUP)]
        totals = [sums[s] + part for s, part in zip(group, partials(group, last))]
        for s, total in zip(group, totals):
            if first > 0:
                sums[s] = total
        if first == 0:
            for chains in ((0, 1), (2, 3)):
                for half, part in enumerate((slice(0, middle), slice(middle, packed))):
                    for chain in chains:
                        send(chain, 0, half, totals[chain][part])

    for step in range(1, 4):
        for chains in ((0, 1), (2, 3)):
            for half in range(2):
                for chain in chains:
                    if step < len(CHAINS[chain][1]):
                        s = pair_at(CHAINS[chain][1][step])
                        send(chain, step, half, sums[s, halves[half]] + arrived(chain, step - 1, half))

    lane = lax.broadcasted_iota(jnp.int32, gift.shape, 1)
    spread = jnp.zeros(gift.shape, F32)

    def added(terms):
        return jnp.sum(jnp.sum(terms, axis=0, keepdims=True), axis=1, keepdims=True)

    def scales(place):
        return (
            scale[place, :LANES, :LANES], scale[place, LANES:, :LANES], scale[place, LANES:, LANES:]
        )

    for place, (long_chain, short_chain) in enumerate(((0, 3), (1, 2))):
        s = 2 * aux_me + place
        for half in range(2):
            sums[s, halves[half]] = (
                sums[s, halves[half]] + arrived(short_chain, 2, half) + arrived(long_chain, 3, half)
            )
        low, left_low = sums[s, :LANES], sums[s, LANES:pnos]
        right_up, high = sums[s, pnos:pnos + over], sums[s, pnos + over:, :over]
        scale_low, scale_side, scale_high = scales(place)
        mixed = left_low * (left_low - right_up) + right_up * right_up
        energy = 0.5 * (
            added((2.0 * low - low.T) * low * scale_low)
            + added((2.0 * high - high.T) * high * scale_high)
            + added(2.0 * mixed * scale_side)
        )
        hits = (lane == own_slot_of(s)).astype(F32) + (lane == slot_of(s)).astype(F32)
        spread = spread + hits * energy

    gift[...] = spread
    gifts[1, aux_me] = spread
    passes = []
    for distance in range(aux_size):
        for side, target in enumerate((right, occ_me, left)):
            if side == 1 and distance == 0:
                continue
            passed = pltpu.make_async_remote_copy(
                src_ref=gift,
                dst_ref=gifts.at[side, aux_me],
                send_sem=gift_send.at[side, distance],
                recv_sem=gift_recv.at[side, distance],
                device_id=(target, aux_at(distance)),
                device_id_type=MESH,
            )
            passed.start()
            passes.append(passed)

    for place in range(2):
        s = 2 * aux_me + place
        scale_low, scale_side, scale_high = scales(place)
        amp[place, :LANES, :LANES] = sums[s, :LANES] * scale_low
        amp[place, LANES:, :LANES] = sums[s, LANES:pnos] * scale_side
        amp[place, :LANES, LANES:] = (sums[s, pnos:pnos + over] * scale_side).T
        amp[place, LANES:, LANES:] = (sums[s, pnos + over:, :over] * scale_high).T

    for passed in passes:
        passed.wait_recv()
    from_left, own, from_right = (
        functools.reduce(lambda a, b: a + b, [gifts[side, z] for z in range(aux_size)])
        for side in range(3)
    )
    orb_out[...] = (
        pltpu.roll(from_left, LANES - 2 * orbs, 1)
        + pltpu.roll(own, LANES - orbs, 1)
        + from_right
    )

    for move in moves:
        move.wait_send()
    for message in messages.values():
        message.wait_send()
    for passed in passes:
        passed.wait_send()


def shards(mesh, ao_blocks, pno_coef, pno_energy, occ_energy, pair_partner, pno_count):
    orbs, virtuals, aux_block = ao_blocks.shape
    pairs, _, pnos = pno_coef.shape
    occ_size, aux_size = mesh.shape["occ"], mesh.shape["aux"]
    rows = -(-pnos // 16) * 16
    padded = -(-pnos // LANES) * LANES
    packed = pnos + 2 * (pnos - LANES)
    share = pairs // aux_size
    chunks = len(WIDTHS)
    vmem = pl.BlockSpec(memory_space=pltpu.VMEM)
    anywhere = pl.BlockSpec(memory_space=pl.ANY)
    dma = pltpu.SemaphoreType.DMA
    amplitudes, orbital = pl.pallas_call(
        functools.partial(kernel, occ_size, aux_size),
        out_shape=(
            jax.ShapeDtypeStruct((share, pnos, pnos), F32),
            jax.ShapeDtypeStruct((8, LANES), F32),
        ),
        in_specs=[anywhere] * 6,
        out_specs=(vmem, vmem),
        scratch_shapes=[
            pltpu.SMEM((pairs,), jnp.int32),
            pltpu.SMEM((pairs,), jnp.int32),
            pltpu.SMEM(occ_energy.shape, F32),
            pltpu.VMEM((pairs, pnos), F32),
            pltpu.VMEM((pairs, pnos, virtuals), BF16),
            pltpu.VMEM((pairs, rows, virtuals), BF16),
            pltpu.VMEM((pairs, padded, aux_block), BF16),
            pltpu.VMEM((pairs, packed, LANES), F32),
            pltpu.VMEM((MESSAGES, packed, LANES), BF16),
            pltpu.VMEM((MESSAGES, packed, LANES), BF16),
            pltpu.VMEM((share, pnos, pnos), F32),
            pltpu.VMEM((8, LANES), F32),
            pltpu.VMEM((3, aux_size, 8, LANES), F32),
        ]
        + [pltpu.VMEM((3 * orbs, virtuals, width), BF16) for width in WIDTHS]
        + [
            dma((5,)),
            dma((chunks,)),
            dma((2, chunks)),
            dma((2, chunks)),
            dma((MESSAGES, 2)),
            dma((MESSAGES, 2)),
            dma((3, aux_size)),
            dma((3, aux_size)),
        ],
        compiler_params=pltpu.CompilerParams(
            collective_id=0, has_side_effects=True, vmem_limit_bytes=48 * 1024 * 1024
        ),
    )(
        *(
            pltpu.with_memory_space_constraint(x, pltpu.HBM)
            for x in (
                pair_partner, pno_count, occ_energy, pno_energy, ao_blocks,
                jnp.swapaxes(pno_coef, 1, 2),
            )
        )
    )
    return amplitudes, orbital[0, :orbs]


def solution(mesh):
    return jax.shard_map(
        functools.partial(shards, mesh),
        mesh=mesh,
        in_specs=(
            P("occ", None, "aux"),
            P("occ", None, None),
            P("occ", None),
            P(),
            P("occ"),
            P("occ"),
        ),
        out_specs=(P(("occ", "aux"), None, None), P("occ")),
        check_vma=False,
    )
```

```python
import functools

import jax
import jax.numpy as jnp
from jax import lax
from jax.experimental import pallas as pl
from jax.experimental.pallas import tpu as pltpu
from jax.sharding import PartitionSpec as P

MESH = pl.DeviceIdType.MESH
WIDTHS = (256, 256, 256, 128, 128)
GROUP = 4
LANES = 128
F32 = jnp.float32
BF16 = jnp.bfloat16

ORDER = (
    (4, 0), (4, 1), (3, 1), (-3, 0),
    (3, 0), (-3, 1), (2, 0), (-2, 1),
    (2, 1), (-2, 0), (1, 0), (-1, 1),
    (1, 1), (-1, 0), (0, 0), (0, 1),
)
CHAINS = (
    (1, (0, 4, 6, 10)),
    (-1, (1, 5, 7, 11)),
    (1, (2, 8, 12)),
    (-1, (3, 9, 13)),
)
MESSAGES = 14


def nt_dot(left, right):
    return lax.dot_general(
        left, right, (((1,), (1,)), ((), ())), preferred_element_type=F32
    )


def kernel(
    occ_size, aux_size, partner_in, counts_in, occ_energy_in, energies_in, ao, coef,
    amp, orb_out,
    partner, counts, occ_energy, energies, coef_raw, coef_t, own_proj, sums, parcel, landed, scale, corners, gift, gifts, *rest,
):
    windows = rest[:len(WIDTHS)]
    (
        small_sem, local_sem, ao_send, ao_recv, chain_send, chain_recv,
        gift_send, gift_recv,
    ) = rest[len(WIDTHS):]
    starts = [sum(WIDTHS[:k]) for k in range(len(WIDTHS))]
    occ_me, aux_me = lax.axis_index("occ"), lax.axis_index("aux")
    right = lax.rem(occ_me + 1, occ_size)
    left = lax.rem(occ_me + occ_size - 1, occ_size)
    orbs = ao.shape[0]
    virtuals = ao.shape[1]
    pairs, pnos, _ = coef.shape
    per_orbital = pairs // orbs
    padded = own_proj.shape[1]
    rows = -(-pnos // 16) * 16
    over = pnos - LANES
    fold, tail = LANES // 2, pnos + over
    strip = over - fold
    low_lanes = lax.broadcasted_iota(jnp.int32, (fold // 2, LANES), 1) < fold

    def aux_at(distance):
        return lax.rem(aux_me + distance + aux_size, aux_size)

    barrier = pltpu.get_barrier_semaphore()
    for place in ((left, aux_me), (right, aux_me), (occ_me, aux_at(1)), (occ_me, aux_at(-1))):
        pl.semaphore_signal(barrier, inc=1, device_id=place, device_id_type=MESH)

    pl.semaphore_wait(barrier, 4)

    moves = []
    for k, (start, width) in enumerate(zip(starts, WIDTHS)):
        for side, (target, slot) in enumerate(((right, 0), (left, 2 * orbs))):
            move = pltpu.make_async_remote_copy(
                src_ref=ao.at[:, :, pl.ds(start, width)],
                dst_ref=windows[k].at[pl.ds(slot, orbs)],
                send_sem=ao_send.at[side],
                recv_sem=ao_recv.at[side, k],
                device_id=(target, aux_me),
                device_id_type=MESH,
            )
            move.start()
            moves.append(move)

    smalls = []
    for number, (source, target) in enumerate((
        (counts_in, counts), (partner_in, partner), (occ_energy_in, occ_energy),
        (energies_in, energies), (coef, coef_raw),
    )):
        small = pltpu.make_async_copy(source, target, small_sem.at[number])
        small.start()
        smalls.append(small)
    fetches = []
    for k, (start, width) in enumerate(zip(starts, WIDTHS)):
        fetch = pltpu.make_async_copy(
            ao.at[:, :, pl.ds(start, width)],
            windows[k].at[pl.ds(orbs, orbs)],
            local_sem.at[k],
        )
        fetch.start()
        fetches.append(fetch)

    for small in smalls:
        small.wait()
    whole_rows = pnos // 16 * 16
    places = lax.broadcasted_iota(jnp.int32, (pnos, virtuals), 0)

    def mask(s, carry):
        kept = jnp.where(places < counts[s], coef_raw[s].astype(F32), 0.0)
        coef_t[s, whole_rows:] = jnp.zeros((rows - whole_rows, virtuals), BF16)
        coef_t[s, :pnos] = kept.astype(BF16)
        own_proj[s, rows:] = jnp.zeros((padded - rows, own_proj.shape[2]), BF16)
        return carry

    lax.fori_loop(0, pairs, mask, 0)

    first_slot = (occ_me - 1) * orbs

    def slot_of(s):
        return jnp.clip(partner[s] - first_slot, 0, 3 * orbs - 1)

    def own_slot_of(s):
        return orbs + s // per_orbital

    for place in range(2):
        s = 2 * aux_me + place
        shift = occ_energy[first_slot + own_slot_of(s)] + occ_energy[partner[s]]
        row = jnp.broadcast_to(energies[pl.ds(s, 1), :], (pnos, pnos))
        scale[place] = -1.0 / (row + row.T - shift)

    for k, (start, width) in enumerate(zip(starts, WIDTHS)):
        fetches[k].wait()

        def project(o, carry):
            block = windows[k][orbs + o]
            turned = coef_t[pl.ds(o * per_orbital, per_orbital)]
            own = jnp.dot(
                turned.reshape(per_orbital * rows, virtuals), block, preferred_element_type=F32
            )
            own = own.astype(BF16).reshape(per_orbital, rows, width)
            own_proj[pl.ds(o * per_orbital, per_orbital), :rows, start:start + width] = own
            return carry

        lax.fori_loop(0, orbs, project, 0)

    def pack(top, rest, strip_rows):
        corner = rest[:, LANES:]
        folded = jnp.where(
            low_lanes, corner[:fold // 2], pltpu.roll(corner[fold // 2:fold], fold, 1)
        )
        return jnp.concatenate(
            [top[:pnos], rest[:over, :LANES], folded, corner[fold:over], strip_rows[16 - (rows - pnos) - strip:16 - (rows - pnos)]],
            axis=0,
        )

    def unpack_corner(low_rows, last_rows, strip_rows):
        turned = jnp.concatenate(
            [low_rows, pltpu.roll(low_rows, fold, 1), last_rows], axis=0
        ).T
        bottom = pltpu.roll(strip_rows, LANES - (LANES - rows + LANES), 1)
        return jnp.concatenate([turned[:fold], bottom[:, :over]], axis=0)

    def partials(group, k):
        start, width = starts[k], WIDTHS[k]
        others = [
            jnp.dot(coef_t[s], windows[k][slot_of(s)], preferred_element_type=F32).astype(BF16)
            for s in group
        ]
        owns = [own_proj[s, :, start:start + width] for s in group]
        tops = [nt_dot(own[:rows], other[:LANES]) for own, other in zip(owns, others)]
        rests = [nt_dot(other[LANES:], own) for own, other in zip(owns, others)]
        strips = [nt_dot(own[rows - 16:rows], other[rows - LANES:]) for own, other in zip(owns, others)]
        return [pack(*terms) for terms in zip(tops, rests, strips)]

    def arrive(k):
        moves[2 * k].wait_recv()
        moves[2 * k + 1].wait_recv()

    last = len(WIDTHS) - 1
    for k in range(last):
        arrive(k)

        def accumulate(number, carry):
            group = [GROUP * number + i for i in range(GROUP)]
            for s, part in zip(group, partials(group, k)):
                sums[s] = part if k == 0 else sums[s] + part
            return carry

        lax.fori_loop(0, pairs // GROUP, accumulate, 0)

    def pair_at(position):
        distance, place = ORDER[position]
        return 2 * aux_at(distance) + place

    messages = {}

    def number_of(chain, step):
        return sum(len(CHAINS[c][1]) for c in range(chain)) + step

    packed = sums.shape[1]
    middle = -(-packed // 32) * 16
    halves = (pl.ds(0, middle), pl.ds(middle, packed - middle))

    def send(chain, step, half, total):
        number = number_of(chain, step)
        parcel[number, halves[half]] = total.astype(BF16)
        message = pltpu.make_async_remote_copy(
            src_ref=parcel.at[number, halves[half]],
            dst_ref=landed.at[number, halves[half]],
            send_sem=chain_send,
            recv_sem=chain_recv.at[number, half],
            device_id=(occ_me, aux_at(CHAINS[chain][0])),
            device_id_type=MESH,
        )
        message.start()
        messages[chain, step, half] = message

    def arrived(chain, step, half):
        messages[chain, step, half].wait_recv()
        return landed[number_of(chain, step), halves[half]].astype(F32)

    arrive(last)
    for first in range(0, pairs, GROUP):
        group = [pair_at(position) for position in range(first, first + GROUP)]
        totals = [sums[s] + part for s, part in zip(group, partials(group, last))]
        for s, total in zip(group, totals):
            if first > 0:
                sums[s] = total
        if first == 0:
            for chains in ((0, 1), (2, 3)):
                for half, part in enumerate((slice(0, middle), slice(middle, packed))):
                    for chain in chains:
                        send(chain, 0, half, totals[chain][part])

    for step in range(1, 4):
        for chains in ((0, 1), (2, 3)):
            for half in range(2):
                for chain in chains:
                    if step < len(CHAINS[chain][1]):
                        s = pair_at(CHAINS[chain][1][step])
                        send(chain, step, half, sums[s, halves[half]] + arrived(chain, step - 1, half))

    lane = lax.broadcasted_iota(jnp.int32, gift.shape, 1)
    spread = jnp.zeros(gift.shape, F32)

    def added(terms):
        return jnp.sum(jnp.sum(terms, axis=0, keepdims=True), axis=1, keepdims=True)

    def scales(place):
        return (
            scale[place, :LANES, :LANES], scale[place, LANES:, :LANES], scale[place, LANES:, LANES:]
        )

    for place, (long_chain, short_chain) in enumerate(((0, 3), (1, 2))):
        s = 2 * aux_me + place
        for half in range(2):
            sums[s, halves[half]] = (
                sums[s, halves[half]] + arrived(short_chain, 2, half) + arrived(long_chain, 3, half)
            )
        low, left_low, right_up = sums[s, :LANES], sums[s, LANES:pnos], sums[s, pnos:tail]
        high = unpack_corner(
            sums[s, tail:tail + fold // 2],
            sums[s, tail + fold // 2:tail + fold // 2 + strip],
            sums[s, tail + fold // 2 + strip:],
        )
        corners[place] = high
        scale_low, scale_side, scale_high = scales(place)
        mixed = left_low * (left_low - right_up) + right_up * right_up
        energy = 0.5 * (
            added((2.0 * low - low.T) * low * scale_low)
            + added((2.0 * high - high.T) * high * scale_high)
            + added(2.0 * mixed * scale_side)
        )
        hits = (lane == own_slot_of(s)).astype(F32) + (lane == slot_of(s)).astype(F32)
        spread = spread + hits * energy

    gift[...] = spread
    gifts[aux_size + aux_me] = spread
    for distance in range(aux_size):
        for side, target in enumerate((right, occ_me, left)):
            if side == 1 and distance == 0:
                continue
            passed = pltpu.make_async_remote_copy(
                src_ref=gift,
                dst_ref=gifts.at[side * aux_size + aux_me],
                send_sem=gift_send,
                recv_sem=gift_recv,
                device_id=(target, aux_at(distance)),
                device_id_type=MESH,
            )
            passed.start()
    others = gifts.at[pl.ds(0, 3 * aux_size - 1)]
    all_passed = pltpu.make_async_remote_copy(
        src_ref=others,
        dst_ref=others,
        send_sem=gift_send,
        recv_sem=gift_recv,
        device_id=(right, aux_me),
        device_id_type=MESH,
    )

    for place in range(2):
        s = 2 * aux_me + place
        scale_low, scale_side, scale_high = scales(place)
        amp[place, :LANES, :LANES] = sums[s, :LANES] * scale_low
        amp[place, LANES:, :LANES] = sums[s, LANES:pnos] * scale_side
        amp[place, :LANES, LANES:] = (sums[s, pnos:tail] * scale_side).T
        amp[place, LANES:, LANES:] = corners[place] * scale_high

    all_passed.wait_recv()
    from_left, own, from_right = (
        functools.reduce(lambda a, b: a + b, [gifts[side * aux_size + z] for z in range(aux_size)])
        for side in range(3)
    )
    orb_out[...] = (
        pltpu.roll(from_left, LANES - 2 * orbs, 1)
        + pltpu.roll(own, LANES - orbs, 1)
        + from_right
    )

    for side in range(2):
        pltpu.make_async_remote_copy(
            src_ref=ao,
            dst_ref=ao,
            send_sem=ao_send.at[side],
            recv_sem=ao_recv.at[side, 0],
            device_id=(right, aux_me),
            device_id_type=MESH,
        ).wait_send()
    pltpu.make_async_remote_copy(
        src_ref=parcel,
        dst_ref=landed,
        send_sem=chain_send,
        recv_sem=chain_recv.at[0, 0],
        device_id=(right, aux_me),
        device_id_type=MESH,
    ).wait_send()
    all_passed.wait_send()


def shards(mesh, ao_blocks, pno_coef, pno_energy, occ_energy, pair_partner, pno_count):
    orbs, virtuals, aux_block = ao_blocks.shape
    pairs, _, pnos = pno_coef.shape
    occ_size, aux_size = mesh.shape["occ"], mesh.shape["aux"]
    rows = -(-pnos // 16) * 16
    padded = -(-pnos // LANES) * LANES
    packed = pnos + (pnos - LANES) + LANES // 4 + 2 * (pnos - LANES - LANES // 2)
    share = pairs // aux_size
    chunks = len(WIDTHS)
    vmem = pl.BlockSpec(memory_space=pltpu.VMEM)
    anywhere = pl.BlockSpec(memory_space=pl.ANY)
    dma = pltpu.SemaphoreType.DMA
    amplitudes, orbital = pl.pallas_call(
        functools.partial(kernel, occ_size, aux_size),
        out_shape=(
            jax.ShapeDtypeStruct((share, pnos, pnos), F32),
            jax.ShapeDtypeStruct((8, LANES), F32),
        ),
        in_specs=[anywhere] * 6,
        out_specs=(vmem, vmem),
        scratch_shapes=[
            pltpu.SMEM((pairs,), jnp.int32),
            pltpu.SMEM((pairs,), jnp.int32),
            pltpu.SMEM(occ_energy.shape, F32),
            pltpu.VMEM((pairs, pnos), F32),
            pltpu.VMEM((pairs, pnos, virtuals), BF16),
            pltpu.VMEM((pairs, rows, virtuals), BF16),
            pltpu.VMEM((pairs, padded, aux_block), BF16),
            pltpu.VMEM((pairs, packed, LANES), F32),
            pltpu.VMEM((MESSAGES, packed, LANES), BF16),
            pltpu.VMEM((MESSAGES, packed, LANES), BF16),
            pltpu.VMEM((share, pnos, pnos), F32),
            pltpu.VMEM((share, pnos - LANES, pnos - LANES), F32),
            pltpu.VMEM((8, LANES), F32),
            pltpu.VMEM((3 * aux_size, 8, LANES), F32),
        ]
        + [pltpu.VMEM((3 * orbs, virtuals, width), BF16) for width in WIDTHS]
        + [
            dma((5,)),
            dma((chunks,)),
            dma((2,)),
            dma((2, chunks)),
            dma,
            dma((MESSAGES, 2)),
            dma,
            dma,
        ],
        compiler_params=pltpu.CompilerParams(
            collective_id=0, has_side_effects=True, vmem_limit_bytes=48 * 1024 * 1024
        ),
    )(
        *(
            pltpu.with_memory_space_constraint(x, pltpu.HBM)
            for x in (
                pair_partner, pno_count, occ_energy, pno_energy, ao_blocks,
                jnp.swapaxes(pno_coef, 1, 2),
            )
        )
    )
    return amplitudes, orbital[0, :orbs]


def solution(mesh):
    return jax.shard_map(
        functools.partial(shards, mesh),
        mesh=mesh,
        in_specs=(
            P("occ", None, "aux"),
            P("occ", None, None),
            P("occ", None),
            P(),
            P("occ"),
            P("occ"),
        ),
        out_specs=(P(("occ", "aux"), None, None), P("occ")),
        check_vma=False,
    )
```

```python
import functools

import jax
import jax.numpy as jnp
from jax import lax
from jax.experimental import pallas as pl
from jax.experimental.pallas import tpu as pltpu
from jax.sharding import PartitionSpec as P

MESH = pl.DeviceIdType.MESH
WIDTHS = (256, 256, 256, 128, 128)
GROUP = 4
LANES = 128
F32 = jnp.float32
BF16 = jnp.bfloat16

ORDER = (
    (4, 0), (4, 1), (3, 1), (-3, 0),
    (3, 0), (-3, 1), (2, 0), (-2, 1),
    (2, 1), (-2, 0), (1, 0), (-1, 1),
    (1, 1), (-1, 0), (0, 0), (0, 1),
)
CHAINS = (
    (1, (0, 4, 6, 10)),
    (-1, (1, 5, 7, 11)),
    (1, (2, 8, 12)),
    (-1, (3, 9, 13)),
)
MESSAGES = 14


def nt_dot(left, right):
    return lax.dot_general(
        left, right, (((1,), (1,)), ((), ())), preferred_element_type=F32
    )


def kernel(
    occ_size, aux_size, partner_in, counts_in, occ_energy_in, energies_in, ao, coef,
    amp, orb_out,
    partner, counts, occ_energy, energies, coef_raw, coef_t, own_proj, sums, parcel, landed, scale, corners, gift, gifts, *rest,
):
    windows = rest[:len(WIDTHS)]
    (
        small_sem, local_sem, ao_send, ao_recv, chain_send, chain_recv,
        gift_send, gift_recv, ready,
    ) = rest[len(WIDTHS):]
    starts = [sum(WIDTHS[:k]) for k in range(len(WIDTHS))]
    occ_me, aux_me = lax.axis_index("occ"), lax.axis_index("aux")
    right = lax.rem(occ_me + 1, occ_size)
    left = lax.rem(occ_me + occ_size - 1, occ_size)
    orbs = ao.shape[0]
    virtuals = ao.shape[1]
    pairs, pnos, _ = coef.shape
    per_orbital = pairs // orbs
    padded = own_proj.shape[1]
    rows = -(-pnos // 16) * 16
    over = pnos - LANES
    fold, tail = LANES // 2, pnos + over
    strip = over - fold
    low_lanes = lax.broadcasted_iota(jnp.int32, (fold // 2, LANES), 1) < fold

    def aux_at(distance):
        return lax.rem(aux_me + distance + aux_size, aux_size)

    top = aux_size - 1
    first_occ, last_occ = occ_me == 0, occ_me == occ_size - 1
    barrier = pltpu.get_barrier_semaphore()

    def announce(semaphore, occ_place, aux_place):
        pl.semaphore_signal(
            semaphore, inc=1, device_id=(occ_place, aux_place), device_id_type=MESH
        )

    pl.when(jnp.logical_not(first_occ))(lambda: announce(barrier, left, aux_me))
    pl.when(jnp.logical_not(last_occ))(lambda: announce(barrier, right, aux_me))

    @pl.when(aux_me < top)
    def _():
        announce(barrier, occ_me, aux_at(1))

    @pl.when(aux_me == 0)
    def _():
        announce(barrier, occ_me, aux_at(-1))

    beside = (occ_me + occ_size - 1) // occ_size + (2 * occ_size - 2 - occ_me) // occ_size
    pl.semaphore_wait(barrier, beside + (aux_me + top) // aux_size + aux_me // top)

    moves = []
    for k, (start, width) in enumerate(zip(starts, WIDTHS)):
        for side, (target, slot) in enumerate(((right, 0), (left, 2 * orbs))):
            move = pltpu.make_async_remote_copy(
                src_ref=ao.at[:, :, pl.ds(start, width)],
                dst_ref=windows[k].at[pl.ds(slot, orbs)],
                send_sem=ao_send.at[side],
                recv_sem=ao_recv.at[side, k],
                device_id=(target, aux_me),
                device_id_type=MESH,
            )
            moves.append(move)
            stand_in = pltpu.make_async_copy(
                ao.at[:, :, pl.ds(start, width)],
                windows[k].at[pl.ds(slot, orbs)],
                ao_recv.at[side, k],
            )
            goes, lacks = ((last_occ, first_occ), (first_occ, last_occ))[side]
            pl.when(jnp.logical_not(goes))(move.start)
            pl.when(lacks)(stand_in.start)

    @pl.when(aux_me > 0)
    def _():
        announce(ready, occ_me, aux_at(-1))

    @pl.when(aux_me == top)
    def _():
        announce(ready, occ_me, aux_at(1))

    smalls = []
    for number, (source, target) in enumerate((
        (counts_in, counts), (partner_in, partner), (occ_energy_in, occ_energy),
        (energies_in, energies), (coef, coef_raw),
    )):
        small = pltpu.make_async_copy(source, target, small_sem.at[number])
        small.start()
        smalls.append(small)
    fetches = []
    for k, (start, width) in enumerate(zip(starts, WIDTHS)):
        fetch = pltpu.make_async_copy(
            ao.at[:, :, pl.ds(start, width)],
            windows[k].at[pl.ds(orbs, orbs)],
            local_sem.at[k],
        )
        fetch.start()
        fetches.append(fetch)

    for small in smalls:
        small.wait()
    whole_rows = pnos // 16 * 16
    places = lax.broadcasted_iota(jnp.int32, (pnos, virtuals), 0)

    for side, lacks in ((0, first_occ), (2, last_occ)):
        @pl.when(lacks)
        def _():
            for z in range(aux_size):
                gifts[side * aux_size + z] = jnp.zeros(gift.shape, F32)

    def mask(s, carry):
        kept = jnp.where(places < counts[s], coef_raw[s].astype(F32), 0.0)
        coef_t[s, whole_rows:] = jnp.zeros((rows - whole_rows, virtuals), BF16)
        coef_t[s, :pnos] = kept.astype(BF16)
        own_proj[s, rows:] = jnp.zeros((padded - rows, own_proj.shape[2]), BF16)
        return carry

    lax.fori_loop(0, pairs, mask, 0)

    first_slot = (occ_me - 1) * orbs

    def slot_of(s):
        return jnp.clip(partner[s] - first_slot, 0, 3 * orbs - 1)

    def own_slot_of(s):
        return orbs + s // per_orbital

    for place in range(2):
        s = 2 * aux_me + place
        shift = occ_energy[first_slot + own_slot_of(s)] + occ_energy[partner[s]]
        row = jnp.broadcast_to(energies[pl.ds(s, 1), :], (pnos, pnos))
        scale[place] = -1.0 / (row + row.T - shift)

    for k, (start, width) in enumerate(zip(starts, WIDTHS)):
        fetches[k].wait()

        def project(o, carry):
            block = windows[k][orbs + o]
            turned = coef_t[pl.ds(o * per_orbital, per_orbital)]
            own = jnp.dot(
                turned.reshape(per_orbital * rows, virtuals), block, preferred_element_type=F32
            )
            own = own.astype(BF16).reshape(per_orbital, rows, width)
            own_proj[pl.ds(o * per_orbital, per_orbital), :rows, start:start + width] = own
            return carry

        lax.fori_loop(0, orbs, project, 0)

    def pack(top, rest, strip_rows):
        corner = rest[:, LANES:]
        folded = jnp.where(
            low_lanes, corner[:fold // 2], pltpu.roll(corner[fold // 2:fold], fold, 1)
        )
        return jnp.concatenate(
            [top[:pnos], rest[:over, :LANES], folded, corner[fold:over], strip_rows[16 - (rows - pnos) - strip:16 - (rows - pnos)]],
            axis=0,
        )

    def unpack_corner(low_rows, last_rows, strip_rows):
        turned = jnp.concatenate(
            [low_rows, pltpu.roll(low_rows, fold, 1), last_rows], axis=0
        ).T
        bottom = pltpu.roll(strip_rows, LANES - (LANES - rows + LANES), 1)
        return jnp.concatenate([turned[:fold], bottom[:, :over]], axis=0)

    def partials(group, k):
        start, width = starts[k], WIDTHS[k]
        others = [
            jnp.dot(coef_t[s], windows[k][slot_of(s)], preferred_element_type=F32).astype(BF16)
            for s in group
        ]
        owns = [own_proj[s, :, start:start + width] for s in group]
        tops = [nt_dot(own[:rows], other[:LANES]) for own, other in zip(owns, others)]
        rests = [nt_dot(other[LANES:], own) for own, other in zip(owns, others)]
        strips = [nt_dot(own[rows - 16:rows], other[rows - LANES:]) for own, other in zip(owns, others)]
        return [pack(*terms) for terms in zip(tops, rests, strips)]

    def arrive(k):
        moves[2 * k].wait_recv()
        moves[2 * k + 1].wait_recv()

    last = len(WIDTHS) - 1
    for k in range(last):
        arrive(k)

        def accumulate(number, carry):
            group = [GROUP * number + i for i in range(GROUP)]
            for s, part in zip(group, partials(group, k)):
                sums[s] = part if k == 0 else sums[s] + part
            return carry

        lax.fori_loop(0, pairs // GROUP, accumulate, 0)

    def pair_at(position):
        distance, place = ORDER[position]
        return 2 * aux_at(distance) + place

    messages = {}

    def number_of(chain, step):
        return sum(len(CHAINS[c][1]) for c in range(chain)) + step

    packed = sums.shape[1]
    middle = -(-packed // 32) * 16
    halves = (pl.ds(0, middle), pl.ds(middle, packed - middle))

    def send(chain, step, half, total):
        number = number_of(chain, step)
        parcel[number, halves[half]] = total.astype(BF16)
        message = pltpu.make_async_remote_copy(
            src_ref=parcel.at[number, halves[half]],
            dst_ref=landed.at[number, halves[half]],
            send_sem=chain_send,
            recv_sem=chain_recv.at[number, half],
            device_id=(occ_me, aux_at(CHAINS[chain][0])),
            device_id_type=MESH,
        )
        message.start()
        messages[chain, step, half] = message

    def arrived(chain, step, half):
        messages[chain, step, half].wait_recv()
        return landed[number_of(chain, step), halves[half]].astype(F32)

    @pl.when(jnp.logical_and(aux_me > 0, aux_me < top))
    def _():
        pl.semaphore_wait(ready, 1)

    @pl.when(aux_me == 0)
    def _():
        pl.semaphore_wait(ready, 2)

    arrive(last)
    for first in range(0, pairs, GROUP):
        group = [pair_at(position) for position in range(first, first + GROUP)]
        totals = [sums[s] + part for s, part in zip(group, partials(group, last))]
        for s, total in zip(group, totals):
            if first > 0:
                sums[s] = total
        if first == 0:
            for chains in ((0, 1), (2, 3)):
                for half, part in enumerate((slice(0, middle), slice(middle, packed))):
                    for chain in chains:
                        send(chain, 0, half, totals[chain][part])

    for step in range(1, 4):
        for chains in ((0, 1), (2, 3)):
            for half in range(2):
                for chain in chains:
                    if step < len(CHAINS[chain][1]):
                        s = pair_at(CHAINS[chain][1][step])
                        send(chain, step, half, sums[s, halves[half]] + arrived(chain, step - 1, half))

    lane = lax.broadcasted_iota(jnp.int32, gift.shape, 1)
    spread = jnp.zeros(gift.shape, F32)

    def added(terms):
        return jnp.sum(jnp.sum(terms, axis=0, keepdims=True), axis=1, keepdims=True)

    def scales(place):
        return (
            scale[place, :LANES, :LANES], scale[place, LANES:, :LANES], scale[place, LANES:, LANES:]
        )

    for place, (long_chain, short_chain) in enumerate(((0, 3), (1, 2))):
        s = 2 * aux_me + place
        for half in range(2):
            sums[s, halves[half]] = (
                sums[s, halves[half]] + arrived(short_chain, 2, half) + arrived(long_chain, 3, half)
            )
        low, left_low, right_up = sums[s, :LANES], sums[s, LANES:pnos], sums[s, pnos:tail]
        high = unpack_corner(
            sums[s, tail:tail + fold // 2],
            sums[s, tail + fold // 2:tail + fold // 2 + strip],
            sums[s, tail + fold // 2 + strip:],
        )
        corners[place] = high
        scale_low, scale_side, scale_high = scales(place)
        mixed = left_low * (left_low - right_up) + right_up * right_up
        energy = 0.5 * (
            added((2.0 * low - low.T) * low * scale_low)
            + added((2.0 * high - high.T) * high * scale_high)
            + added(2.0 * mixed * scale_side)
        )
        hits = (lane == own_slot_of(s)).astype(F32) + (lane == slot_of(s)).astype(F32)
        spread = spread + hits * energy

    gift[...] = spread
    gifts[aux_size + aux_me] = spread
    lacking = (first_occ, None, last_occ)
    barred = (last_occ, None, first_occ)

    def unless(condition, action):
        if condition is None:
            action()
        else:
            pl.when(jnp.logical_not(condition))(action)

    for distance in range(aux_size):
        for side, target in enumerate((right, occ_me, left)):
            if side == 1 and distance == 0:
                continue
            passed = pltpu.make_async_remote_copy(
                src_ref=gift,
                dst_ref=gifts.at[side * aux_size + aux_me],
                send_sem=gift_send.at[side],
                recv_sem=gift_recv.at[side],
                device_id=(target, aux_at(distance)),
                device_id_type=MESH,
            )
            unless(barred[side], passed.start)
    passes = []
    for side in range(3):
        several = gifts.at[pl.ds(0, aux_size - (side == 1))]
        passes.append(
            pltpu.make_async_remote_copy(
                src_ref=several,
                dst_ref=several,
                send_sem=gift_send.at[side],
                recv_sem=gift_recv.at[side],
                device_id=(right, aux_me),
                device_id_type=MESH,
            )
        )

    for place in range(2):
        s = 2 * aux_me + place
        scale_low, scale_side, scale_high = scales(place)
        amp[place, :LANES, :LANES] = sums[s, :LANES] * scale_low
        amp[place, LANES:, :LANES] = sums[s, LANES:pnos] * scale_side
        amp[place, :LANES, LANES:] = (sums[s, pnos:tail] * scale_side).T
        amp[place, LANES:, LANES:] = corners[place] * scale_high

    for side, passed in enumerate(passes):
        unless(lacking[side], passed.wait_recv)
    from_left, own, from_right = (
        functools.reduce(lambda a, b: a + b, [gifts[side * aux_size + z] for z in range(aux_size)])
        for side in range(3)
    )
    orb_out[...] = (
        pltpu.roll(from_left, LANES - 2 * orbs, 1)
        + pltpu.roll(own, LANES - orbs, 1)
        + from_right
    )

    for side, goes in enumerate((last_occ, first_occ)):
        moved = pltpu.make_async_remote_copy(
            src_ref=ao,
            dst_ref=ao,
            send_sem=ao_send.at[side],
            recv_sem=ao_recv.at[side, 0],
            device_id=(right, aux_me),
            device_id_type=MESH,
        )
        unless(goes, moved.wait_send)
    pltpu.make_async_remote_copy(
        src_ref=parcel,
        dst_ref=landed,
        send_sem=chain_send,
        recv_sem=chain_recv.at[0, 0],
        device_id=(right, aux_me),
        device_id_type=MESH,
    ).wait_send()
    for side, passed in enumerate(passes):
        unless(barred[side], passed.wait_send)


def shards(mesh, ao_blocks, pno_coef, pno_energy, occ_energy, pair_partner, pno_count):
    orbs, virtuals, aux_block = ao_blocks.shape
    pairs, _, pnos = pno_coef.shape
    occ_size, aux_size = mesh.shape["occ"], mesh.shape["aux"]
    rows = -(-pnos // 16) * 16
    padded = -(-pnos // LANES) * LANES
    packed = pnos + (pnos - LANES) + LANES // 4 + 2 * (pnos - LANES - LANES // 2)
    share = pairs // aux_size
    chunks = len(WIDTHS)
    vmem = pl.BlockSpec(memory_space=pltpu.VMEM)
    anywhere = pl.BlockSpec(memory_space=pl.ANY)
    dma = pltpu.SemaphoreType.DMA
    amplitudes, orbital = pl.pallas_call(
        functools.partial(kernel, occ_size, aux_size),
        out_shape=(
            jax.ShapeDtypeStruct((share, pnos, pnos), F32),
            jax.ShapeDtypeStruct((8, LANES), F32),
        ),
        in_specs=[anywhere] * 6,
        out_specs=(vmem, vmem),
        scratch_shapes=[
            pltpu.SMEM((pairs,), jnp.int32),
            pltpu.SMEM((pairs,), jnp.int32),
            pltpu.SMEM(occ_energy.shape, F32),
            pltpu.VMEM((pairs, pnos), F32),
            pltpu.VMEM((pairs, pnos, virtuals), BF16),
            pltpu.VMEM((pairs, rows, virtuals), BF16),
            pltpu.VMEM((pairs, padded, aux_block), BF16),
            pltpu.VMEM((pairs, packed, LANES), F32),
            pltpu.VMEM((MESSAGES, packed, LANES), BF16),
            pltpu.VMEM((MESSAGES, packed, LANES), BF16),
            pltpu.VMEM((share, pnos, pnos), F32),
            pltpu.VMEM((share, pnos - LANES, pnos - LANES), F32),
            pltpu.VMEM((8, LANES), F32),
            pltpu.VMEM((3 * aux_size, 8, LANES), F32),
        ]
        + [pltpu.VMEM((3 * orbs, virtuals, width), BF16) for width in WIDTHS]
        + [
            dma((5,)),
            dma((chunks,)),
            dma((2,)),
            dma((2, chunks)),
            dma,
            dma((MESSAGES, 2)),
            dma((3,)),
            dma((3,)),
            pltpu.SemaphoreType.REGULAR,
        ],
        compiler_params=pltpu.CompilerParams(
            collective_id=0, has_side_effects=True, vmem_limit_bytes=48 * 1024 * 1024
        ),
    )(
        *(
            pltpu.with_memory_space_constraint(x, pltpu.HBM)
            for x in (
                pair_partner, pno_count, occ_energy, pno_energy, ao_blocks,
                jnp.swapaxes(pno_coef, 1, 2),
            )
        )
    )
    return amplitudes, orbital[0, :orbs]


def solution(mesh):
    return jax.shard_map(
        functools.partial(shards, mesh),
        mesh=mesh,
        in_specs=(
            P("occ", None, "aux"),
            P("occ", None, None),
            P("occ", None),
            P(),
            P("occ"),
            P("occ"),
        ),
        out_specs=(P(("occ", "aux"), None, None), P("occ")),
        check_vma=False,
    )
```

```python
import functools

import jax
import jax.numpy as jnp
from jax import lax
from jax.experimental import pallas as pl
from jax.experimental.pallas import tpu as pltpu
from jax.sharding import PartitionSpec as P

MESH = pl.DeviceIdType.MESH
WIDTHS = (256, 256, 256, 128, 128, 128)
FINAL, OWN_LOAN, BORROWED = 3, 4, 5
LENDERS = 2
GROUP = 4
LANES = 128
F32 = jnp.float32
BF16 = jnp.bfloat16

ORDER = (
    (4, 0), (4, 1), (3, 1), (-3, 0),
    (3, 0), (-3, 1), (2, 0), (-2, 1),
    (2, 1), (-2, 0), (1, 0), (-1, 1),
    (1, 1), (-1, 0), (0, 0), (0, 1),
)
CHAINS = (
    (1, (0, 4, 6, 10)),
    (-1, (1, 5, 7, 11)),
    (1, (2, 8, 12)),
    (-1, (3, 9, 13)),
)
MESSAGES = 14


def nt_dot(left, right):
    return lax.dot_general(
        left, right, (((1,), (1,)), ((), ())), preferred_element_type=F32
    )


def kernel(
    occ_size, aux_size, partner_in, counts_in, occ_energy_in, energies_in, ao, coef,
    amp, orb_out,
    partner, counts, occ_energy, energies, coef_raw, coef_t, own_proj, sums, parcel, landed, scale, corners, gift, gifts, *rest,
):
    windows = rest[:len(WIDTHS)]
    (
        small_sem, local_sem, ao_send, ao_recv, loan_sem, chain_send, chain_recv,
        gift_send, gift_recv, ready,
    ) = rest[len(WIDTHS):]
    starts = [sum(WIDTHS[:k]) for k in range(len(WIDTHS))]
    occ_me, aux_me = lax.axis_index("occ"), lax.axis_index("aux")
    right = lax.rem(occ_me + 1, occ_size)
    left = lax.rem(occ_me + occ_size - 1, occ_size)
    orbs = ao.shape[0]
    virtuals = ao.shape[1]
    pairs, pnos, _ = coef.shape
    per_orbital = pairs // orbs
    padded = own_proj.shape[1]
    rows = -(-pnos // 16) * 16
    over = pnos - LANES
    fold, tail = LANES // 2, pnos + over
    strip = over - fold
    low_lanes = lax.broadcasted_iota(jnp.int32, (fold // 2, LANES), 1) < fold

    def aux_at(distance):
        return lax.rem(aux_me + distance + aux_size, aux_size)

    top = aux_size - 1
    first_occ, last_occ = occ_me == 0, occ_me == occ_size - 1
    barrier = pltpu.get_barrier_semaphore()

    def announce(semaphore, occ_place, aux_place):
        pl.semaphore_signal(
            semaphore, inc=1, device_id=(occ_place, aux_place), device_id_type=MESH
        )

    pl.when(jnp.logical_not(first_occ))(lambda: announce(barrier, left, aux_me))
    pl.when(jnp.logical_not(last_occ))(lambda: announce(barrier, right, aux_me))

    @pl.when(aux_me < top)
    def _():
        announce(barrier, occ_me, aux_at(1))

    late, early = aux_me > top - LENDERS, aux_me < LENDERS

    @pl.when(early)
    def _():
        announce(barrier, occ_me, top - aux_me)

    beside = (occ_me + occ_size - 1) // occ_size + (2 * occ_size - 2 - occ_me) // occ_size
    pl.semaphore_wait(barrier, beside + (aux_me + top) // aux_size + (aux_me + LENDERS) // aux_size)

    def source_of(k):
        if k == BORROWED:
            return windows[k].at[pl.ds(orbs, orbs)]
        return ao.at[:, :, pl.ds(starts[k], WIDTHS[k])]

    def move(k, side):
        target, slot = ((right, 0), (left, 2 * orbs))[side]
        return pltpu.make_async_remote_copy(
            src_ref=source_of(k),
            dst_ref=windows[k].at[pl.ds(slot, orbs)],
            send_sem=ao_send.at[side, max(k, FINAL) - FINAL],
            recv_sem=ao_recv.at[side, k],
            device_id=(target, aux_me),
            device_id_type=MESH,
        )

    def start_moves(k):
        for side, slot in enumerate((0, 2 * orbs)):
            stand_in = pltpu.make_async_copy(
                source_of(k), windows[k].at[pl.ds(slot, orbs)], ao_recv.at[side, k]
            )
            goes, lacks = ((last_occ, first_occ), (first_occ, last_occ))[side]
            pl.when(jnp.logical_not(goes))(move(k, side).start)
            pl.when(lacks)(stand_in.start)

    loan = pltpu.make_async_remote_copy(
        src_ref=source_of(OWN_LOAN),
        dst_ref=windows[BORROWED].at[pl.ds(orbs, orbs)],
        send_sem=loan_sem.at[0],
        recv_sem=loan_sem.at[1],
        device_id=(occ_me, top - aux_me),
        device_id_type=MESH,
    )
    for k in range(FINAL):
        start_moves(k)
    pl.when(late)(loan.start)
    pl.when(jnp.logical_not(late))(lambda: start_moves(OWN_LOAN))
    pl.when(jnp.logical_not(early))(lambda: start_moves(FINAL))

    @pl.when(aux_me > 0)
    def _():
        announce(ready, occ_me, aux_at(-1))

    @pl.when(aux_me == top)
    def _():
        announce(ready, occ_me, aux_at(1))

    smalls = []
    for number, (source, target) in enumerate((
        (counts_in, counts), (partner_in, partner), (occ_energy_in, occ_energy),
        (energies_in, energies), (coef, coef_raw),
    )):
        small = pltpu.make_async_copy(source, target, small_sem.at[number])
        small.start()
        smalls.append(small)
    fetches = []
    for k in range(BORROWED):
        fetch = pltpu.make_async_copy(
            source_of(k), windows[k].at[pl.ds(orbs, orbs)], local_sem.at[k]
        )
        fetch.start()
        fetches.append(fetch)

    for small in smalls:
        small.wait()
    whole_rows = pnos // 16 * 16
    places = lax.broadcasted_iota(jnp.int32, (pnos, virtuals), 0)

    for side, lacks in ((0, first_occ), (2, last_occ)):
        @pl.when(lacks)
        def _():
            for z in range(aux_size):
                gifts[side * aux_size + z] = jnp.zeros(gift.shape, F32)

    def mask(s, carry):
        kept = jnp.where(places < counts[s], coef_raw[s].astype(F32), 0.0)
        coef_t[s, whole_rows:] = jnp.zeros((rows - whole_rows, virtuals), BF16)
        coef_t[s, :pnos] = kept.astype(BF16)
        own_proj[s, rows:] = jnp.zeros((padded - rows, own_proj.shape[2]), BF16)
        return carry

    lax.fori_loop(0, pairs, mask, 0)

    first_slot = (occ_me - 1) * orbs

    def slot_of(s):
        return jnp.clip(partner[s] - first_slot, 0, 3 * orbs - 1)

    def own_slot_of(s):
        return orbs + s // per_orbital

    for place in range(2):
        s = 2 * aux_me + place
        shift = occ_energy[first_slot + own_slot_of(s)] + occ_energy[partner[s]]
        row = jnp.broadcast_to(energies[pl.ds(s, 1), :], (pnos, pnos))
        scale[place] = -1.0 / (row + row.T - shift)

    def project(k):
        start, width = starts[k], WIDTHS[k]

        def of_orbital(o, carry):
            block = windows[k][orbs + o]
            turned = coef_t[pl.ds(o * per_orbital, per_orbital)]
            own = jnp.dot(
                turned.reshape(per_orbital * rows, virtuals), block, preferred_element_type=F32
            )
            own = own.astype(BF16).reshape(per_orbital, rows, width)
            own_proj[pl.ds(o * per_orbital, per_orbital), :rows, start:start + width] = own
            return carry

        lax.fori_loop(0, orbs, of_orbital, 0)

    for k in range(BORROWED):
        fetches[k].wait()
        if k == OWN_LOAN:
            pl.when(jnp.logical_not(late))(lambda: project(OWN_LOAN))
        else:
            project(k)

    def pack(top, rest, strip_rows):
        corner = rest[:, LANES:]
        folded = jnp.where(
            low_lanes, corner[:fold // 2], pltpu.roll(corner[fold // 2:fold], fold, 1)
        )
        return jnp.concatenate(
            [top[:pnos], rest[:over, :LANES], folded, corner[fold:over], strip_rows[16 - (rows - pnos) - strip:16 - (rows - pnos)]],
            axis=0,
        )

    def unpack_corner(low_rows, last_rows, strip_rows):
        turned = jnp.concatenate(
            [low_rows, pltpu.roll(low_rows, fold, 1), last_rows], axis=0
        ).T
        bottom = pltpu.roll(strip_rows, LANES - (LANES - rows + LANES), 1)
        return jnp.concatenate([turned[:fold], bottom[:, :over]], axis=0)

    def partials(group, k):
        start, width = starts[k], WIDTHS[k]
        others = [
            jnp.dot(coef_t[s], windows[k][slot_of(s)], preferred_element_type=F32).astype(BF16)
            for s in group
        ]
        owns = [own_proj[s, :, start:start + width] for s in group]
        tops = [nt_dot(own[:rows], other[:LANES]) for own, other in zip(owns, others)]
        rests = [nt_dot(other[LANES:], own) for own, other in zip(owns, others)]
        strips = [nt_dot(own[rows - 16:rows], other[rows - LANES:]) for own, other in zip(owns, others)]
        return [pack(*terms) for terms in zip(tops, rests, strips)]

    def arrive(k):
        for side in range(2):
            move(k, side).wait_recv()

    def add_piece(k):
        arrive(k)

        def accumulate(number, carry):
            group = [GROUP * number + i for i in range(GROUP)]
            for s, part in zip(group, partials(group, k)):
                sums[s] = part if k == 0 else sums[s] + part
            return carry

        lax.fori_loop(0, pairs // GROUP, accumulate, 0)

    add_piece(0)
    add_piece(1)

    @pl.when(early)
    def _():
        loan.wait_recv()
        start_moves(BORROWED)
        start_moves(FINAL)
        project(BORROWED)

    add_piece(2)
    pl.when(jnp.logical_not(late))(lambda: add_piece(OWN_LOAN))
    pl.when(early)(lambda: add_piece(BORROWED))

    def pair_at(position):
        distance, place = ORDER[position]
        return 2 * aux_at(distance) + place

    messages = {}

    def number_of(chain, step):
        return sum(len(CHAINS[c][1]) for c in range(chain)) + step

    packed = sums.shape[1]
    middle = -(-packed // 32) * 16
    halves = (pl.ds(0, middle), pl.ds(middle, packed - middle))

    def send(chain, step, half, total):
        number = number_of(chain, step)
        parcel[number, halves[half]] = total.astype(BF16)
        message = pltpu.make_async_remote_copy(
            src_ref=parcel.at[number, halves[half]],
            dst_ref=landed.at[number, halves[half]],
            send_sem=chain_send,
            recv_sem=chain_recv.at[number, half],
            device_id=(occ_me, aux_at(CHAINS[chain][0])),
            device_id_type=MESH,
        )
        message.start()
        messages[chain, step, half] = message

    def arrived(chain, step, half):
        messages[chain, step, half].wait_recv()
        return landed[number_of(chain, step), halves[half]].astype(F32)

    @pl.when(jnp.logical_and(aux_me > 0, aux_me < top))
    def _():
        pl.semaphore_wait(ready, 1)

    @pl.when(aux_me == 0)
    def _():
        pl.semaphore_wait(ready, 2)

    arrive(FINAL)
    for first in range(0, pairs, GROUP):
        group = [pair_at(position) for position in range(first, first + GROUP)]
        totals = [sums[s] + part for s, part in zip(group, partials(group, FINAL))]
        for s, total in zip(group, totals):
            if first > 0:
                sums[s] = total
        if first == 0:
            for chains in ((0, 1), (2, 3)):
                for half, part in enumerate((slice(0, middle), slice(middle, packed))):
                    for chain in chains:
                        send(chain, 0, half, totals[chain][part])

    for step in range(1, 4):
        for chains in ((0, 1), (2, 3)):
            for half in range(2):
                for chain in chains:
                    if step < len(CHAINS[chain][1]):
                        s = pair_at(CHAINS[chain][1][step])
                        send(chain, step, half, sums[s, halves[half]] + arrived(chain, step - 1, half))

    lane = lax.broadcasted_iota(jnp.int32, gift.shape, 1)
    spread = jnp.zeros(gift.shape, F32)

    def added(terms):
        return jnp.sum(jnp.sum(terms, axis=0, keepdims=True), axis=1, keepdims=True)

    def scales(place):
        return (
            scale[place, :LANES, :LANES], scale[place, LANES:, :LANES], scale[place, LANES:, LANES:]
        )

    for place, (long_chain, short_chain) in enumerate(((0, 3), (1, 2))):
        s = 2 * aux_me + place
        for half in range(2):
            sums[s, halves[half]] = (
                sums[s, halves[half]] + arrived(short_chain, 2, half) + arrived(long_chain, 3, half)
            )
        low, left_low, right_up = sums[s, :LANES], sums[s, LANES:pnos], sums[s, pnos:tail]
        high = unpack_corner(
            sums[s, tail:tail + fold // 2],
            sums[s, tail + fold // 2:tail + fold // 2 + strip],
            sums[s, tail + fold // 2 + strip:],
        )
        corners[place] = high
        scale_low, scale_side, scale_high = scales(place)
        mixed = left_low * (left_low - right_up) + right_up * right_up
        energy = 0.5 * (
            added((2.0 * low - low.T) * low * scale_low)
            + added((2.0 * high - high.T) * high * scale_high)
            + added(2.0 * mixed * scale_side)
        )
        hits = (lane == own_slot_of(s)).astype(F32) + (lane == slot_of(s)).astype(F32)
        spread = spread + hits * energy

    gift[...] = spread
    gifts[aux_size + aux_me] = spread
    lacking = (first_occ, None, last_occ)
    barred = (last_occ, None, first_occ)

    def unless(condition, action):
        if condition is None:
            action()
        else:
            pl.when(jnp.logical_not(condition))(action)

    for distance in range(aux_size):
        for side, target in enumerate((right, occ_me, left)):
            if side == 1 and distance == 0:
                continue
            passed = pltpu.make_async_remote_copy(
                src_ref=gift,
                dst_ref=gifts.at[side * aux_size + aux_me],
                send_sem=gift_send.at[side],
                recv_sem=gift_recv.at[side],
                device_id=(target, aux_at(distance)),
                device_id_type=MESH,
            )
            unless(barred[side], passed.start)
    passes = []
    for side in range(3):
        several = gifts.at[pl.ds(0, aux_size - (side == 1))]
        passes.append(
            pltpu.make_async_remote_copy(
                src_ref=several,
                dst_ref=several,
                send_sem=gift_send.at[side],
                recv_sem=gift_recv.at[side],
                device_id=(right, aux_me),
                device_id_type=MESH,
            )
        )

    for place in range(2):
        s = 2 * aux_me + place
        scale_low, scale_side, scale_high = scales(place)
        amp[place, :LANES, :LANES] = sums[s, :LANES] * scale_low
        amp[place, LANES:, :LANES] = sums[s, LANES:pnos] * scale_side
        amp[place, :LANES, LANES:] = (sums[s, pnos:tail] * scale_side).T
        amp[place, LANES:, LANES:] = corners[place] * scale_high

    for side, passed in enumerate(passes):
        unless(lacking[side], passed.wait_recv)
    from_left, own, from_right = (
        functools.reduce(lambda a, b: a + b, [gifts[side * aux_size + z] for z in range(aux_size)])
        for side in range(3)
    )
    orb_out[...] = (
        pltpu.roll(from_left, LANES - 2 * orbs, 1)
        + pltpu.roll(own, LANES - orbs, 1)
        + from_right
    )

    for side, goes in enumerate((last_occ, first_occ)):
        main = ao.at[:, :, pl.ds(0, starts[OWN_LOAN])]
        moved = pltpu.make_async_remote_copy(
            src_ref=main,
            dst_ref=main,
            send_sem=ao_send.at[side, 0],
            recv_sem=ao_recv.at[side, 0],
            device_id=(right, aux_me),
            device_id_type=MESH,
        )
        stays = jnp.logical_not(goes)
        pl.when(stays)(moved.wait_send)
        pl.when(jnp.logical_and(stays, jnp.logical_not(late)))(move(OWN_LOAN, side).wait_send)
        pl.when(jnp.logical_and(stays, early))(move(BORROWED, side).wait_send)
    pl.when(late)(loan.wait_send)
    pltpu.make_async_remote_copy(
        src_ref=parcel,
        dst_ref=landed,
        send_sem=chain_send,
        recv_sem=chain_recv.at[0, 0],
        device_id=(right, aux_me),
        device_id_type=MESH,
    ).wait_send()
    for side, passed in enumerate(passes):
        unless(barred[side], passed.wait_send)


def shards(mesh, ao_blocks, pno_coef, pno_energy, occ_energy, pair_partner, pno_count):
    orbs, virtuals, _ = ao_blocks.shape
    pairs, _, pnos = pno_coef.shape
    occ_size, aux_size = mesh.shape["occ"], mesh.shape["aux"]
    rows = -(-pnos // 16) * 16
    padded = -(-pnos // LANES) * LANES
    packed = pnos + (pnos - LANES) + LANES // 4 + 2 * (pnos - LANES - LANES // 2)
    share = pairs // aux_size
    chunks = len(WIDTHS)
    vmem = pl.BlockSpec(memory_space=pltpu.VMEM)
    anywhere = pl.BlockSpec(memory_space=pl.ANY)
    dma = pltpu.SemaphoreType.DMA
    amplitudes, orbital = pl.pallas_call(
        functools.partial(kernel, occ_size, aux_size),
        out_shape=(
            jax.ShapeDtypeStruct((share, pnos, pnos), F32),
            jax.ShapeDtypeStruct((8, LANES), F32),
        ),
        in_specs=[anywhere] * 6,
        out_specs=(vmem, vmem),
        scratch_shapes=[
            pltpu.SMEM((pairs,), jnp.int32),
            pltpu.SMEM((pairs,), jnp.int32),
            pltpu.SMEM(occ_energy.shape, F32),
            pltpu.VMEM((pairs, pnos), F32),
            pltpu.VMEM((pairs, pnos, virtuals), BF16),
            pltpu.VMEM((pairs, rows, virtuals), BF16),
            pltpu.VMEM((pairs, padded, sum(WIDTHS)), BF16),
            pltpu.VMEM((pairs, packed, LANES), F32),
            pltpu.VMEM((MESSAGES, packed, LANES), BF16),
            pltpu.VMEM((MESSAGES, packed, LANES), BF16),
            pltpu.VMEM((share, pnos, pnos), F32),
            pltpu.VMEM((share, pnos - LANES, pnos - LANES), F32),
            pltpu.VMEM((8, LANES), F32),
            pltpu.VMEM((3 * aux_size, 8, LANES), F32),
        ]
        + [pltpu.VMEM((3 * orbs, virtuals, width), BF16) for width in WIDTHS]
        + [
            dma((5,)),
            dma((BORROWED,)),
            dma((2, 3)),
            dma((2, chunks)),
            dma((2,)),
            dma,
            dma((MESSAGES, 2)),
            dma((3,)),
            dma((3,)),
            pltpu.SemaphoreType.REGULAR,
        ],
        compiler_params=pltpu.CompilerParams(
            collective_id=0, has_side_effects=True, vmem_limit_bytes=48 * 1024 * 1024
        ),
    )(
        *(
            pltpu.with_memory_space_constraint(x, pltpu.HBM)
            for x in (
                pair_partner, pno_count, occ_energy, pno_energy, ao_blocks,
                jnp.swapaxes(pno_coef, 1, 2),
            )
        )
    )
    return amplitudes, orbital[0, :orbs]


def solution(mesh):
    return jax.shard_map(
        functools.partial(shards, mesh),
        mesh=mesh,
        in_specs=(
            P("occ", None, "aux"),
            P("occ", None, None),
            P("occ", None),
            P(),
            P("occ"),
            P("occ"),
        ),
        out_specs=(P(("occ", "aux"), None, None), P("occ")),
        check_vma=False,
    )
```

```python
import functools

import jax
import jax.numpy as jnp
from jax import lax
from jax.experimental import pallas as pl
from jax.experimental.pallas import tpu as pltpu
from jax.sharding import PartitionSpec as P

MESH = pl.DeviceIdType.MESH
WIDTHS = (256, 256, 256, 128, 128, 128)
FINAL, OWN_LOAN, BORROWED = 3, 4, 5
LENDERS = 2
GROUP = 4
LANES = 128
F32 = jnp.float32
BF16 = jnp.bfloat16

ORDER = (
    (4, 0), (4, 1), (3, 1), (-3, 0),
    (3, 0), (-3, 1), (2, 0), (-2, 1),
    (2, 1), (-2, 0), (1, 0), (-1, 1),
    (1, 1), (-1, 0), (0, 0), (0, 1),
)
CHAINS = (
    (1, (0, 4, 6, 10)),
    (-1, (1, 5, 7, 11)),
    (1, (2, 8, 12)),
    (-1, (3, 9, 13)),
)
MESSAGES = 14


def nt_dot(left, right):
    return lax.dot_general(
        left, right, (((1,), (1,)), ((), ())), preferred_element_type=F32
    )


def kernel(
    occ_size, aux_size, partner_in, counts_in, occ_energy_in, energies_in, ao, coef,
    amp, orb_out,
    partner, counts, occ_energy, energies, coef_raw, coef_t, own_proj, sums, parcel, landed, scale, corners, gift, gifts, *rest,
):
    windows = rest[:len(WIDTHS)]
    (
        small_sem, local_sem, ao_send, ao_recv, loan_sem, chain_send, chain_recv,
        gift_send, gift_recv, ready,
    ) = rest[len(WIDTHS):]
    starts = [sum(WIDTHS[:k]) for k in range(len(WIDTHS))]
    occ_me, aux_me = lax.axis_index("occ"), lax.axis_index("aux")
    right = lax.rem(occ_me + 1, occ_size)
    left = lax.rem(occ_me + occ_size - 1, occ_size)
    orbs = ao.shape[0]
    virtuals = ao.shape[1]
    pairs, pnos, _ = coef.shape
    per_orbital = pairs // orbs
    padded = own_proj.shape[1]
    rows = -(-pnos // 16) * 16
    over = pnos - LANES
    fold, tail = LANES // 2, pnos + over
    strip = over - fold
    low_lanes = lax.broadcasted_iota(jnp.int32, (fold // 2, LANES), 1) < fold

    def aux_at(distance):
        return lax.rem(aux_me + distance + aux_size, aux_size)

    top = aux_size - 1
    first_occ, last_occ = occ_me == 0, occ_me == occ_size - 1
    barrier = pltpu.get_barrier_semaphore()

    def announce(semaphore, occ_place, aux_place):
        pl.semaphore_signal(
            semaphore, inc=1, device_id=(occ_place, aux_place), device_id_type=MESH
        )

    pl.when(jnp.logical_not(first_occ))(lambda: announce(barrier, left, aux_me))
    pl.when(jnp.logical_not(last_occ))(lambda: announce(barrier, right, aux_me))

    @pl.when(aux_me < top)
    def _():
        announce(barrier, occ_me, aux_at(1))

    late, early = aux_me > top - LENDERS, aux_me < LENDERS

    @pl.when(early)
    def _():
        announce(barrier, occ_me, top - aux_me)

    beside = (occ_me + occ_size - 1) // occ_size + (2 * occ_size - 2 - occ_me) // occ_size
    pl.semaphore_wait(barrier, beside + (aux_me + top) // aux_size + (aux_me + LENDERS) // aux_size)

    def source_of(k):
        if k == BORROWED:
            return windows[k].at[pl.ds(orbs, orbs)]
        return ao.at[:, :, pl.ds(starts[k], WIDTHS[k])]

    def move(k, side):
        target, slot = ((right, 0), (left, 2 * orbs))[side]
        return pltpu.make_async_remote_copy(
            src_ref=source_of(k),
            dst_ref=windows[k].at[pl.ds(slot, orbs)],
            send_sem=ao_send.at[side, max(k, FINAL) - FINAL],
            recv_sem=ao_recv.at[side, k],
            device_id=(target, aux_me),
            device_id_type=MESH,
        )

    def start_moves(k):
        for side, slot in enumerate((0, 2 * orbs)):
            stand_in = pltpu.make_async_copy(
                source_of(k), windows[k].at[pl.ds(slot, orbs)], ao_recv.at[side, k]
            )
            goes, lacks = ((last_occ, first_occ), (first_occ, last_occ))[side]
            pl.when(jnp.logical_not(goes))(move(k, side).start)
            pl.when(lacks)(stand_in.start)

    loan = pltpu.make_async_remote_copy(
        src_ref=source_of(OWN_LOAN),
        dst_ref=windows[BORROWED].at[pl.ds(orbs, orbs)],
        send_sem=loan_sem.at[0],
        recv_sem=loan_sem.at[1],
        device_id=(occ_me, top - aux_me),
        device_id_type=MESH,
    )
    for k in range(FINAL):
        start_moves(k)
    pl.when(late)(loan.start)
    pl.when(jnp.logical_not(late))(lambda: start_moves(OWN_LOAN))
    start_moves(FINAL)

    @pl.when(aux_me > 0)
    def _():
        announce(ready, occ_me, aux_at(-1))

    @pl.when(aux_me == top)
    def _():
        announce(ready, occ_me, aux_at(1))

    smalls = []
    for number, (source, target) in enumerate((
        (counts_in, counts), (partner_in, partner), (occ_energy_in, occ_energy),
        (energies_in, energies), (coef, coef_raw),
    )):
        small = pltpu.make_async_copy(source, target, small_sem.at[number])
        small.start()
        smalls.append(small)
    fetches = []
    for k in range(BORROWED):
        fetch = pltpu.make_async_copy(
            source_of(k), windows[k].at[pl.ds(orbs, orbs)], local_sem.at[k]
        )
        fetch.start()
        fetches.append(fetch)

    for small in smalls:
        small.wait()
    whole_rows = pnos // 16 * 16
    places = lax.broadcasted_iota(jnp.int32, (pnos, virtuals), 0)

    for side, lacks in ((0, first_occ), (2, last_occ)):
        @pl.when(lacks)
        def _():
            for z in range(aux_size):
                gifts[side * aux_size + z] = jnp.zeros(gift.shape, F32)

    def mask(s, carry):
        kept = jnp.where(places < counts[s], coef_raw[s].astype(F32), 0.0)
        coef_t[s, whole_rows:] = jnp.zeros((rows - whole_rows, virtuals), BF16)
        coef_t[s, :pnos] = kept.astype(BF16)
        own_proj[s, rows:] = jnp.zeros((padded - rows, own_proj.shape[2]), BF16)
        return carry

    lax.fori_loop(0, pairs, mask, 0)

    first_slot = (occ_me - 1) * orbs

    def slot_of(s):
        return jnp.clip(partner[s] - first_slot, 0, 3 * orbs - 1)

    def own_slot_of(s):
        return orbs + s // per_orbital

    for place in range(2):
        s = 2 * aux_me + place
        shift = occ_energy[first_slot + own_slot_of(s)] + occ_energy[partner[s]]
        row = jnp.broadcast_to(energies[pl.ds(s, 1), :], (pnos, pnos))
        scale[place] = -1.0 / (row + row.T - shift)

    def project(k):
        start, width = starts[k], WIDTHS[k]

        def of_orbital(o, carry):
            block = windows[k][orbs + o]
            turned = coef_t[pl.ds(o * per_orbital, per_orbital)]
            own = jnp.dot(
                turned.reshape(per_orbital * rows, virtuals), block, preferred_element_type=F32
            )
            own = own.astype(BF16).reshape(per_orbital, rows, width)
            own_proj[pl.ds(o * per_orbital, per_orbital), :rows, start:start + width] = own
            return carry

        lax.fori_loop(0, orbs, of_orbital, 0)

    for k in range(BORROWED):
        fetches[k].wait()
        if k == OWN_LOAN:
            pl.when(jnp.logical_not(late))(lambda: project(OWN_LOAN))
        else:
            project(k)

    def pack(top, rest, strip_rows):
        corner = rest[:, LANES:]
        folded = jnp.where(
            low_lanes, corner[:fold // 2], pltpu.roll(corner[fold // 2:fold], fold, 1)
        )
        return jnp.concatenate(
            [top[:pnos], rest[:over, :LANES], folded, corner[fold:over], strip_rows[16 - (rows - pnos) - strip:16 - (rows - pnos)]],
            axis=0,
        )

    def unpack_corner(low_rows, last_rows, strip_rows):
        turned = jnp.concatenate(
            [low_rows, pltpu.roll(low_rows, fold, 1), last_rows], axis=0
        ).T
        bottom = pltpu.roll(strip_rows, LANES - (LANES - rows + LANES), 1)
        return jnp.concatenate([turned[:fold], bottom[:, :over]], axis=0)

    def partials(group, k):
        start, width = starts[k], WIDTHS[k]
        others = [
            jnp.dot(coef_t[s], windows[k][slot_of(s)], preferred_element_type=F32).astype(BF16)
            for s in group
        ]
        owns = [own_proj[s, :, start:start + width] for s in group]
        tops = [nt_dot(own[:rows], other[:LANES]) for own, other in zip(owns, others)]
        rests = [nt_dot(other[LANES:], own) for own, other in zip(owns, others)]
        strips = [nt_dot(own[rows - 16:rows], other[rows - LANES:]) for own, other in zip(owns, others)]
        return [pack(*terms) for terms in zip(tops, rests, strips)]

    def arrive(k):
        for side in range(2):
            move(k, side).wait_recv()

    def add_piece(k):
        arrive(k)

        def accumulate(number, carry):
            group = [GROUP * number + i for i in range(GROUP)]
            for s, part in zip(group, partials(group, k)):
                sums[s] = part if k == 0 else sums[s] + part
            return carry

        lax.fori_loop(0, pairs // GROUP, accumulate, 0)

    add_piece(0)
    add_piece(1)
    add_piece(2)

    @pl.when(early)
    def _():
        loan.wait_recv()
        start_moves(BORROWED)
        project(BORROWED)

    pl.when(jnp.logical_not(late))(lambda: add_piece(OWN_LOAN))
    pl.when(early)(lambda: add_piece(FINAL))

    def pair_at(position):
        distance, place = ORDER[position]
        return 2 * aux_at(distance) + place

    def number_of(chain, step):
        return sum(len(CHAINS[c][1]) for c in range(chain)) + step

    packed = sums.shape[1]
    middle = -(-packed // 32) * 16
    halves = (pl.ds(0, middle), pl.ds(middle, packed - middle))

    def message(chain, step, half):
        number = number_of(chain, step)
        return pltpu.make_async_remote_copy(
            src_ref=parcel.at[number, halves[half]],
            dst_ref=landed.at[number, halves[half]],
            send_sem=chain_send,
            recv_sem=chain_recv.at[number, half],
            device_id=(occ_me, aux_at(CHAINS[chain][0])),
            device_id_type=MESH,
        )

    def send(chain, step, half, total):
        parcel[number_of(chain, step), halves[half]] = total.astype(BF16)
        message(chain, step, half).start()

    def arrived(chain, step, half):
        message(chain, step, half).wait_recv()
        return landed[number_of(chain, step), halves[half]].astype(F32)

    @pl.when(jnp.logical_and(aux_me > 0, aux_me < top))
    def _():
        pl.semaphore_wait(ready, 1)

    @pl.when(aux_me == 0)
    def _():
        pl.semaphore_wait(ready, 2)

    def start_chains(k):
        arrive(k)
        for first, size_of in ((0, 2), (2, 2), *((i, GROUP) for i in range(GROUP, pairs, GROUP))):
            group = [pair_at(position) for position in range(first, first + size_of)]
            totals = [sums[s] + part for s, part in zip(group, partials(group, k))]
            if first >= GROUP:
                for s, total in zip(group, totals):
                    sums[s] = total
            else:
                for half, part in enumerate((slice(0, middle), slice(middle, packed))):
                    for i in range(size_of):
                        send(first + i, 0, half, totals[i][part])

    pl.when(early)(lambda: start_chains(BORROWED))
    pl.when(jnp.logical_not(early))(lambda: start_chains(FINAL))

    for step in range(1, 4):
        for chains in ((0, 1), (2, 3)):
            for half in range(2):
                for chain in chains:
                    if step < len(CHAINS[chain][1]):
                        s = pair_at(CHAINS[chain][1][step])
                        send(chain, step, half, sums[s, halves[half]] + arrived(chain, step - 1, half))

    lane = lax.broadcasted_iota(jnp.int32, gift.shape, 1)
    spread = jnp.zeros(gift.shape, F32)

    def added(terms):
        return jnp.sum(jnp.sum(terms, axis=0, keepdims=True), axis=1, keepdims=True)

    def scales(place):
        return (
            scale[place, :LANES, :LANES], scale[place, LANES:, :LANES], scale[place, LANES:, LANES:]
        )

    for place, (long_chain, short_chain) in enumerate(((0, 3), (1, 2))):
        s = 2 * aux_me + place
        for half in range(2):
            sums[s, halves[half]] = (
                sums[s, halves[half]] + arrived(short_chain, 2, half) + arrived(long_chain, 3, half)
            )
        low, left_low, right_up = sums[s, :LANES], sums[s, LANES:pnos], sums[s, pnos:tail]
        high = unpack_corner(
            sums[s, tail:tail + fold // 2],
            sums[s, tail + fold // 2:tail + fold // 2 + strip],
            sums[s, tail + fold // 2 + strip:],
        )
        corners[place] = high
        scale_low, scale_side, scale_high = scales(place)
        mixed = left_low * (left_low - right_up) + right_up * right_up
        energy = 0.5 * (
            added((2.0 * low - low.T) * low * scale_low)
            + added((2.0 * high - high.T) * high * scale_high)
            + added(2.0 * mixed * scale_side)
        )
        hits = (lane == own_slot_of(s)).astype(F32) + (lane == slot_of(s)).astype(F32)
        spread = spread + hits * energy

    gift[...] = spread
    gifts[aux_size + aux_me] = spread
    lacking = (first_occ, None, last_occ)
    barred = (last_occ, None, first_occ)

    def unless(condition, action):
        if condition is None:
            action()
        else:
            pl.when(jnp.logical_not(condition))(action)

    for distance in range(aux_size):
        for side, target in enumerate((right, occ_me, left)):
            if side == 1 and distance == 0:
                continue
            passed = pltpu.make_async_remote_copy(
                src_ref=gift,
                dst_ref=gifts.at[side * aux_size + aux_me],
                send_sem=gift_send.at[side],
                recv_sem=gift_recv.at[side],
                device_id=(target, aux_at(distance)),
                device_id_type=MESH,
            )
            unless(barred[side], passed.start)
    passes = []
    for side in range(3):
        several = gifts.at[pl.ds(0, aux_size - (side == 1))]
        passes.append(
            pltpu.make_async_remote_copy(
                src_ref=several,
                dst_ref=several,
                send_sem=gift_send.at[side],
                recv_sem=gift_recv.at[side],
                device_id=(right, aux_me),
                device_id_type=MESH,
            )
        )

    for place in range(2):
        s = 2 * aux_me + place
        scale_low, scale_side, scale_high = scales(place)
        amp[place, :LANES, :LANES] = sums[s, :LANES] * scale_low
        amp[place, LANES:, :LANES] = sums[s, LANES:pnos] * scale_side
        amp[place, :LANES, LANES:] = (sums[s, pnos:tail] * scale_side).T
        amp[place, LANES:, LANES:] = corners[place] * scale_high

    for side, passed in enumerate(passes):
        unless(lacking[side], passed.wait_recv)
    from_left, own, from_right = (
        functools.reduce(lambda a, b: a + b, [gifts[side * aux_size + z] for z in range(aux_size)])
        for side in range(3)
    )
    orb_out[...] = (
        pltpu.roll(from_left, LANES - 2 * orbs, 1)
        + pltpu.roll(own, LANES - orbs, 1)
        + from_right
    )

    for side, goes in enumerate((last_occ, first_occ)):
        main = ao.at[:, :, pl.ds(0, starts[OWN_LOAN])]
        moved = pltpu.make_async_remote_copy(
            src_ref=main,
            dst_ref=main,
            send_sem=ao_send.at[side, 0],
            recv_sem=ao_recv.at[side, 0],
            device_id=(right, aux_me),
            device_id_type=MESH,
        )
        stays = jnp.logical_not(goes)
        pl.when(stays)(moved.wait_send)
        pl.when(jnp.logical_and(stays, jnp.logical_not(late)))(move(OWN_LOAN, side).wait_send)
        pl.when(jnp.logical_and(stays, early))(move(BORROWED, side).wait_send)
    pl.when(late)(loan.wait_send)
    pltpu.make_async_remote_copy(
        src_ref=parcel,
        dst_ref=landed,
        send_sem=chain_send,
        recv_sem=chain_recv.at[0, 0],
        device_id=(right, aux_me),
        device_id_type=MESH,
    ).wait_send()
    for side, passed in enumerate(passes):
        unless(barred[side], passed.wait_send)


def shards(mesh, ao_blocks, pno_coef, pno_energy, occ_energy, pair_partner, pno_count):
    orbs, virtuals, _ = ao_blocks.shape
    pairs, _, pnos = pno_coef.shape
    occ_size, aux_size = mesh.shape["occ"], mesh.shape["aux"]
    rows = -(-pnos // 16) * 16
    padded = -(-pnos // LANES) * LANES
    packed = pnos + (pnos - LANES) + LANES // 4 + 2 * (pnos - LANES - LANES // 2)
    share = pairs // aux_size
    chunks = len(WIDTHS)
    vmem = pl.BlockSpec(memory_space=pltpu.VMEM)
    anywhere = pl.BlockSpec(memory_space=pl.ANY)
    dma = pltpu.SemaphoreType.DMA
    amplitudes, orbital = pl.pallas_call(
        functools.partial(kernel, occ_size, aux_size),
        out_shape=(
            jax.ShapeDtypeStruct((share, pnos, pnos), F32),
            jax.ShapeDtypeStruct((8, LANES), F32),
        ),
        in_specs=[anywhere] * 6,
        out_specs=(vmem, vmem),
        scratch_shapes=[
            pltpu.SMEM((pairs,), jnp.int32),
            pltpu.SMEM((pairs,), jnp.int32),
            pltpu.SMEM(occ_energy.shape, F32),
            pltpu.VMEM((pairs, pnos), F32),
            pltpu.VMEM((pairs, pnos, virtuals), BF16),
            pltpu.VMEM((pairs, rows, virtuals), BF16),
            pltpu.VMEM((pairs, padded, sum(WIDTHS)), BF16),
            pltpu.VMEM((pairs, packed, LANES), F32),
            pltpu.VMEM((MESSAGES, packed, LANES), BF16),
            pltpu.VMEM((MESSAGES, packed, LANES), BF16),
            pltpu.VMEM((share, pnos, pnos), F32),
            pltpu.VMEM((share, pnos - LANES, pnos - LANES), F32),
            pltpu.VMEM((8, LANES), F32),
            pltpu.VMEM((3 * aux_size, 8, LANES), F32),
        ]
        + [pltpu.VMEM((3 * orbs, virtuals, width), BF16) for width in WIDTHS]
        + [
            dma((5,)),
            dma((BORROWED,)),
            dma((2, 3)),
            dma((2, chunks)),
            dma((2,)),
            dma,
            dma((MESSAGES, 2)),
            dma((3,)),
            dma((3,)),
            pltpu.SemaphoreType.REGULAR,
        ],
        compiler_params=pltpu.CompilerParams(
            collective_id=0, has_side_effects=True, vmem_limit_bytes=48 * 1024 * 1024
        ),
    )(
        *(
            pltpu.with_memory_space_constraint(x, pltpu.HBM)
            for x in (
                pair_partner, pno_count, occ_energy, pno_energy, ao_blocks,
                jnp.swapaxes(pno_coef, 1, 2),
            )
        )
    )
    return amplitudes, orbital[0, :orbs]


def solution(mesh):
    return jax.shard_map(
        functools.partial(shards, mesh),
        mesh=mesh,
        in_specs=(
            P("occ", None, "aux"),
            P("occ", None, None),
            P("occ", None),
            P(),
            P("occ"),
            P("occ"),
        ),
        out_specs=(P(("occ", "aux"), None, None), P("occ")),
        check_vma=False,
    )
```

```python
import functools

import jax
import jax.numpy as jnp
from jax import lax
from jax.experimental import pallas as pl
from jax.experimental.pallas import tpu as pltpu
from jax.sharding import PartitionSpec as P

MESH = pl.DeviceIdType.MESH
WIDTHS = (256, 256, 256, 128, 128, 128)
FINAL, OWN_LOAN, BORROWED = 3, 4, 5
LENDERS = 2
GROUP = 4
LANES = 128
F32 = jnp.float32
BF16 = jnp.bfloat16

ORDER = (
    (4, 0), (4, 1), (3, 1), (-3, 0),
    (3, 0), (-3, 1), (2, 0), (-2, 1),
    (2, 1), (-2, 0), (1, 0), (-1, 1),
    (1, 1), (-1, 0), (0, 0), (0, 1),
)
CHAINS = (
    (1, (0, 4, 6, 10)),
    (-1, (1, 5, 7, 11)),
    (1, (2, 8, 12)),
    (-1, (3, 9, 13)),
)
MESSAGES = 14


def nt_dot(left, right):
    return lax.dot_general(
        left, right, (((1,), (1,)), ((), ())), preferred_element_type=F32
    )


def kernel(
    occ_size, aux_size, partner_in, counts_in, occ_energy_in, energies_in, ao, coef,
    amp, orb_out,
    partner, counts, occ_energy, energies, coef_raw, coef_t, own_proj, sums, parcel, landed, scale, corners, gift, gifts, *rest,
):
    windows = rest[:len(WIDTHS)]
    (
        small_sem, local_sem, ao_send, ao_recv, loan_sem, chain_send, chain_recv,
        gift_send, gift_recv, ready,
    ) = rest[len(WIDTHS):]
    starts = [sum(WIDTHS[:k]) for k in range(len(WIDTHS))]
    occ_me, aux_me = lax.axis_index("occ"), lax.axis_index("aux")
    right = lax.rem(occ_me + 1, occ_size)
    left = lax.rem(occ_me + occ_size - 1, occ_size)
    orbs = ao.shape[0]
    virtuals = ao.shape[1]
    pairs, pnos, _ = coef.shape
    per_orbital = pairs // orbs
    padded = own_proj.shape[1]
    rows = -(-pnos // 16) * 16
    over = pnos - LANES
    fold, tail = LANES // 2, pnos + over
    strip = over - fold
    low_lanes = lax.broadcasted_iota(jnp.int32, (fold // 2, LANES), 1) < fold

    def aux_at(distance):
        return lax.rem(aux_me + distance + aux_size, aux_size)

    top = aux_size - 1
    first_occ, last_occ = occ_me == 0, occ_me == occ_size - 1
    barrier = pltpu.get_barrier_semaphore()

    def announce(semaphore, occ_place, aux_place):
        pl.semaphore_signal(
            semaphore, inc=1, device_id=(occ_place, aux_place), device_id_type=MESH
        )

    pl.when(jnp.logical_not(first_occ))(lambda: announce(barrier, left, aux_me))
    pl.when(jnp.logical_not(last_occ))(lambda: announce(barrier, right, aux_me))

    @pl.when(aux_me < top)
    def _():
        announce(barrier, occ_me, aux_at(1))

    late, early = aux_me > top - LENDERS, aux_me < LENDERS

    @pl.when(early)
    def _():
        announce(barrier, occ_me, top - aux_me)

    beside = (occ_me + occ_size - 1) // occ_size + (2 * occ_size - 2 - occ_me) // occ_size
    pl.semaphore_wait(barrier, beside + (aux_me + top) // aux_size + (aux_me + LENDERS) // aux_size)

    def source_of(k):
        if k == BORROWED:
            return windows[k].at[pl.ds(orbs, orbs)]
        return ao.at[:, :, pl.ds(starts[k], WIDTHS[k])]

    def move(k, side):
        target, slot = ((right, 0), (left, 2 * orbs))[side]
        return pltpu.make_async_remote_copy(
            src_ref=source_of(k),
            dst_ref=windows[k].at[pl.ds(slot, orbs)],
            send_sem=ao_send.at[side, max(k, FINAL) - FINAL],
            recv_sem=ao_recv.at[k],
            device_id=(target, aux_me),
            device_id_type=MESH,
        )

    def start_moves(k):
        for side, slot in enumerate((0, 2 * orbs)):
            stand_in = pltpu.make_async_copy(
                source_of(k), windows[k].at[pl.ds(slot, orbs)], ao_recv.at[k]
            )
            goes, lacks = ((last_occ, first_occ), (first_occ, last_occ))[side]
            pl.when(jnp.logical_not(goes))(move(k, side).start)
            pl.when(lacks)(stand_in.start)

    loan = pltpu.make_async_remote_copy(
        src_ref=source_of(OWN_LOAN),
        dst_ref=windows[BORROWED].at[pl.ds(orbs, orbs)],
        send_sem=loan_sem.at[0],
        recv_sem=loan_sem.at[1],
        device_id=(occ_me, top - aux_me),
        device_id_type=MESH,
    )
    for k in range(FINAL):
        start_moves(k)
    pl.when(late)(loan.start)
    pl.when(jnp.logical_not(late))(lambda: start_moves(OWN_LOAN))
    pl.when(jnp.logical_not(early))(lambda: start_moves(FINAL))

    @pl.when(aux_me > 0)
    def _():
        announce(ready, occ_me, aux_at(-1))

    @pl.when(aux_me == top)
    def _():
        announce(ready, occ_me, aux_at(1))

    smalls = []
    for number, (source, target) in enumerate((
        (counts_in, counts), (partner_in, partner), (occ_energy_in, occ_energy),
        (energies_in, energies), (coef, coef_raw),
    )):
        small = pltpu.make_async_copy(source, target, small_sem.at[number])
        small.start()
        smalls.append(small)
    fetches = []
    for k in range(BORROWED):
        fetch = pltpu.make_async_copy(
            source_of(k), windows[k].at[pl.ds(orbs, orbs)], local_sem.at[k]
        )
        fetch.start()
        fetches.append(fetch)

    for small in smalls:
        small.wait()
    whole_rows = pnos // 16 * 16
    places = lax.broadcasted_iota(jnp.int32, (pnos, virtuals), 0)

    for side, lacks in ((0, first_occ), (2, last_occ)):
        @pl.when(lacks)
        def _():
            for z in range(aux_size):
                gifts[side * aux_size + z] = jnp.zeros(gift.shape, F32)

    def mask(s, carry):
        kept = jnp.where(places < counts[s], coef_raw[s].astype(F32), 0.0)
        coef_t[s, whole_rows:] = jnp.zeros((rows - whole_rows, virtuals), BF16)
        coef_t[s, :pnos] = kept.astype(BF16)
        own_proj[s, rows:] = jnp.zeros((padded - rows, own_proj.shape[2]), BF16)
        return carry

    lax.fori_loop(0, pairs, mask, 0)

    first_slot = (occ_me - 1) * orbs

    def slot_of(s):
        return jnp.clip(partner[s] - first_slot, 0, 3 * orbs - 1)

    def own_slot_of(s):
        return orbs + s // per_orbital

    for place in range(2):
        s = 2 * aux_me + place
        shift = occ_energy[first_slot + own_slot_of(s)] + occ_energy[partner[s]]
        row = jnp.broadcast_to(energies[pl.ds(s, 1), :], (pnos, pnos))
        scale[place] = -1.0 / (row + row.T - shift)

    def project(k):
        start, width = starts[k], WIDTHS[k]

        def of_orbital(o, carry):
            block = windows[k][orbs + o]
            turned = coef_t[pl.ds(o * per_orbital, per_orbital)]
            own = jnp.dot(
                turned.reshape(per_orbital * rows, virtuals), block, preferred_element_type=F32
            )
            own = own.astype(BF16).reshape(per_orbital, rows, width)
            own_proj[pl.ds(o * per_orbital, per_orbital), :rows, start:start + width] = own
            return carry

        lax.fori_loop(0, orbs, of_orbital, 0)

    for k in range(BORROWED):
        fetches[k].wait()
        if k == OWN_LOAN:
            pl.when(jnp.logical_not(late))(lambda: project(OWN_LOAN))
        else:
            project(k)

    def pack(top, rest, strip_rows):
        corner = rest[:, LANES:]
        folded = jnp.where(
            low_lanes, corner[:fold // 2], pltpu.roll(corner[fold // 2:fold], fold, 1)
        )
        return jnp.concatenate(
            [top[:pnos], rest[:over, :LANES], folded, corner[fold:over], strip_rows[16 - (rows - pnos) - strip:16 - (rows - pnos)]],
            axis=0,
        )

    def unpack_corner(low_rows, last_rows, strip_rows):
        turned = jnp.concatenate(
            [low_rows, pltpu.roll(low_rows, fold, 1), last_rows], axis=0
        ).T
        bottom = pltpu.roll(strip_rows, LANES - (LANES - rows + LANES), 1)
        return jnp.concatenate([turned[:fold], bottom[:, :over]], axis=0)

    def partials(group, k):
        start, width = starts[k], WIDTHS[k]
        others = [
            jnp.dot(coef_t[s], windows[k][slot_of(s)], preferred_element_type=F32).astype(BF16)
            for s in group
        ]
        owns = [own_proj[s, :, start:start + width] for s in group]
        tops = [nt_dot(own[:rows], other[:LANES]) for own, other in zip(owns, others)]
        rests = [nt_dot(other[LANES:], own) for own, other in zip(owns, others)]
        strips = [nt_dot(own[rows - 16:rows], other[rows - LANES:]) for own, other in zip(owns, others)]
        return [pack(*terms) for terms in zip(tops, rests, strips)]

    def arrive(k):
        both = windows[k].at[pl.ds(0, 2 * orbs)]
        pltpu.make_async_remote_copy(
            src_ref=both,
            dst_ref=both,
            send_sem=ao_send.at[0, 0],
            recv_sem=ao_recv.at[k],
            device_id=(right, aux_me),
            device_id_type=MESH,
        ).wait_recv()

    def add_piece(k):
        arrive(k)

        def accumulate(number, carry):
            group = [GROUP * number + i for i in range(GROUP)]
            for s, part in zip(group, partials(group, k)):
                sums[s] = part if k == 0 else sums[s] + part
            return carry

        lax.fori_loop(0, pairs // GROUP, accumulate, 0)

    add_piece(0)
    add_piece(1)

    @pl.when(early)
    def _():
        loan.wait_recv()
        start_moves(BORROWED)
        start_moves(FINAL)
        project(BORROWED)

    add_piece(2)
    pl.when(jnp.logical_not(late))(lambda: add_piece(OWN_LOAN))
    pl.when(early)(lambda: add_piece(BORROWED))

    def pair_at(position):
        distance, place = ORDER[position]
        return 2 * aux_at(distance) + place

    messages = {}

    def number_of(chain, step):
        return sum(len(CHAINS[c][1]) for c in range(chain)) + step

    packed = sums.shape[1]
    middle = -(-packed // 32) * 16
    halves = (pl.ds(0, middle), pl.ds(middle, packed - middle))

    def send(chain, step, half, total):
        number = number_of(chain, step)
        parcel[number, halves[half]] = total.astype(BF16)
        message = pltpu.make_async_remote_copy(
            src_ref=parcel.at[number, halves[half]],
            dst_ref=landed.at[number, halves[half]],
            send_sem=chain_send,
            recv_sem=chain_recv.at[number, half],
            device_id=(occ_me, aux_at(CHAINS[chain][0])),
            device_id_type=MESH,
        )
        message.start()
        messages[chain, step, half] = message

    def arrived(chain, step, half):
        messages[chain, step, half].wait_recv()
        return landed[number_of(chain, step), halves[half]].astype(F32)

    @pl.when(jnp.logical_and(aux_me > 0, aux_me < top))
    def _():
        pl.semaphore_wait(ready, 1)

    @pl.when(aux_me == 0)
    def _():
        pl.semaphore_wait(ready, 2)

    arrive(FINAL)
    for first in range(0, pairs, GROUP):
        group = [pair_at(position) for position in range(first, first + GROUP)]
        totals = [sums[s] + part for s, part in zip(group, partials(group, FINAL))]
        for s, total in zip(group, totals):
            if first > 0:
                sums[s] = total
        if first == 0:
            for chains in ((0, 1), (2, 3)):
                for half, part in enumerate((slice(0, middle), slice(middle, packed))):
                    for chain in chains:
                        send(chain, 0, half, totals[chain][part])

    for step in range(1, 4):
        for chains in ((0, 1), (2, 3)):
            for half in range(2):
                for chain in chains:
                    if step < len(CHAINS[chain][1]):
                        s = pair_at(CHAINS[chain][1][step])
                        send(chain, step, half, sums[s, halves[half]] + arrived(chain, step - 1, half))

    lane = lax.broadcasted_iota(jnp.int32, gift.shape, 1)
    spread = jnp.zeros(gift.shape, F32)

    def added(terms):
        return jnp.sum(jnp.sum(terms, axis=0, keepdims=True), axis=1, keepdims=True)

    def scales(place):
        return (
            scale[place, :LANES, :LANES], scale[place, LANES:, :LANES], scale[place, LANES:, LANES:]
        )

    for place, (long_chain, short_chain) in enumerate(((0, 3), (1, 2))):
        s = 2 * aux_me + place
        for half in range(2):
            sums[s, halves[half]] = (
                sums[s, halves[half]] + arrived(short_chain, 2, half) + arrived(long_chain, 3, half)
            )
        low, left_low, right_up = sums[s, :LANES], sums[s, LANES:pnos], sums[s, pnos:tail]
        high = unpack_corner(
            sums[s, tail:tail + fold // 2],
            sums[s, tail + fold // 2:tail + fold // 2 + strip],
            sums[s, tail + fold // 2 + strip:],
        )
        corners[place] = high
        scale_low, scale_side, scale_high = scales(place)
        mixed = left_low * (left_low - right_up) + right_up * right_up
        energy = 0.5 * (
            added((2.0 * low - low.T) * low * scale_low)
            + added((2.0 * high - high.T) * high * scale_high)
            + added(2.0 * mixed * scale_side)
        )
        hits = (lane == own_slot_of(s)).astype(F32) + (lane == slot_of(s)).astype(F32)
        spread = spread + hits * energy

    gift[...] = spread
    gifts[aux_size + aux_me] = spread
    lacking = (first_occ, None, last_occ)
    barred = (last_occ, None, first_occ)

    def unless(condition, action):
        if condition is None:
            action()
        else:
            pl.when(jnp.logical_not(condition))(action)

    for distance in range(aux_size):
        for side, target in enumerate((right, occ_me, left)):
            if side == 1 and distance == 0:
                continue
            passed = pltpu.make_async_remote_copy(
                src_ref=gift,
                dst_ref=gifts.at[side * aux_size + aux_me],
                send_sem=gift_send.at[side],
                recv_sem=gift_recv.at[side],
                device_id=(target, aux_at(distance)),
                device_id_type=MESH,
            )
            unless(barred[side], passed.start)
    passes = []
    for side in range(3):
        several = gifts.at[pl.ds(0, aux_size - (side == 1))]
        passes.append(
            pltpu.make_async_remote_copy(
                src_ref=several,
                dst_ref=several,
                send_sem=gift_send.at[side],
                recv_sem=gift_recv.at[side],
                device_id=(right, aux_me),
                device_id_type=MESH,
            )
        )

    for place in range(2):
        s = 2 * aux_me + place
        scale_low, scale_side, scale_high = scales(place)
        amp[place, :LANES, :LANES] = sums[s, :LANES] * scale_low
        amp[place, LANES:, :LANES] = sums[s, LANES:pnos] * scale_side
        amp[place, :LANES, LANES:] = (sums[s, pnos:tail] * scale_side).T
        amp[place, LANES:, LANES:] = corners[place] * scale_high

    for side, passed in enumerate(passes):
        unless(lacking[side], passed.wait_recv)
    from_left, own, from_right = (
        functools.reduce(lambda a, b: a + b, [gifts[side * aux_size + z] for z in range(aux_size)])
        for side in range(3)
    )
    orb_out[...] = (
        pltpu.roll(from_left, LANES - 2 * orbs, 1)
        + pltpu.roll(own, LANES - orbs, 1)
        + from_right
    )

    for side, goes in enumerate((last_occ, first_occ)):
        main = ao.at[:, :, pl.ds(0, starts[OWN_LOAN])]
        moved = pltpu.make_async_remote_copy(
            src_ref=main,
            dst_ref=main,
            send_sem=ao_send.at[side, 0],
            recv_sem=ao_recv.at[0],
            device_id=(right, aux_me),
            device_id_type=MESH,
        )
        stays = jnp.logical_not(goes)
        pl.when(stays)(moved.wait_send)
        pl.when(jnp.logical_and(stays, jnp.logical_not(late)))(move(OWN_LOAN, side).wait_send)
        pl.when(jnp.logical_and(stays, early))(move(BORROWED, side).wait_send)
    pl.when(late)(loan.wait_send)
    pltpu.make_async_remote_copy(
        src_ref=parcel,
        dst_ref=landed,
        send_sem=chain_send,
        recv_sem=chain_recv.at[0, 0],
        device_id=(right, aux_me),
        device_id_type=MESH,
    ).wait_send()
    for side, passed in enumerate(passes):
        unless(barred[side], passed.wait_send)


def shards(mesh, ao_blocks, pno_coef, pno_energy, occ_energy, pair_partner, pno_count):
    orbs, virtuals, _ = ao_blocks.shape
    pairs, _, pnos = pno_coef.shape
    occ_size, aux_size = mesh.shape["occ"], mesh.shape["aux"]
    rows = -(-pnos // 16) * 16
    padded = -(-pnos // LANES) * LANES
    packed = pnos + (pnos - LANES) + LANES // 4 + 2 * (pnos - LANES - LANES // 2)
    share = pairs // aux_size
    chunks = len(WIDTHS)
    vmem = pl.BlockSpec(memory_space=pltpu.VMEM)
    anywhere = pl.BlockSpec(memory_space=pl.ANY)
    dma = pltpu.SemaphoreType.DMA
    amplitudes, orbital = pl.pallas_call(
        functools.partial(kernel, occ_size, aux_size),
        out_shape=(
            jax.ShapeDtypeStruct((share, pnos, pnos), F32),
            jax.ShapeDtypeStruct((1, LANES), F32),
        ),
        in_specs=[anywhere] * 6,
        out_specs=(vmem, vmem),
        scratch_shapes=[
            pltpu.SMEM((pairs,), jnp.int32),
            pltpu.SMEM((pairs,), jnp.int32),
            pltpu.SMEM(occ_energy.shape, F32),
            pltpu.VMEM((pairs, pnos), F32),
            pltpu.VMEM((pairs, pnos, virtuals), BF16),
            pltpu.VMEM((pairs, rows, virtuals), BF16),
            pltpu.VMEM((pairs, padded, sum(WIDTHS)), BF16),
            pltpu.VMEM((pairs, packed, LANES), F32),
            pltpu.VMEM((MESSAGES, packed, LANES), BF16),
            pltpu.VMEM((MESSAGES, packed, LANES), BF16),
            pltpu.VMEM((share, pnos, pnos), F32),
            pltpu.VMEM((share, pnos - LANES, pnos - LANES), F32),
            pltpu.VMEM((1, LANES), F32),
            pltpu.VMEM((3 * aux_size, 1, LANES), F32),
        ]
        + [pltpu.VMEM((3 * orbs, virtuals, width), BF16) for width in WIDTHS]
        + [
            dma((5,)),
            dma((BORROWED,)),
            dma((2, 3)),
            dma((chunks,)),
            dma((2,)),
            dma,
            dma((MESSAGES, 2)),
            dma((3,)),
            dma((3,)),
            pltpu.SemaphoreType.REGULAR,
        ],
        compiler_params=pltpu.CompilerParams(
            collective_id=0, has_side_effects=True, vmem_limit_bytes=48 * 1024 * 1024
        ),
    )(
        *(
            pltpu.with_memory_space_constraint(x, pltpu.HBM)
            for x in (
                pair_partner, pno_count, occ_energy, pno_energy, ao_blocks,
                jnp.swapaxes(pno_coef, 1, 2),
            )
        )
    )
    return amplitudes, orbital[0, :orbs]


def solution(mesh):
    return jax.shard_map(
        functools.partial(shards, mesh),
        mesh=mesh,
        in_specs=(
            P("occ", None, "aux"),
            P("occ", None, None),
            P("occ", None),
            P(),
            P("occ"),
            P("occ"),
        ),
        out_specs=(P(("occ", "aux"), None, None), P("occ")),
        check_vma=False,
    )
```
